32 devices in a mesh: grp: 4 (over x, core), pts: 8 (over z, y).
Axes of the slice: x: 2, y: 2, z: 4, core: 2. Of those that a mesh axis runs over, the one named last changes fastest.
Arguments:
- points: float32 [8192, 2048], P(('grp', 'pts')), may hold values from -2 to 2
- log_factor: float32 [8192, 256], P(('grp', 'pts')), may hold values from -40 to 320
- masses: float32 [8192], P(('grp', 'pts')), may hold values from 0.1 to 12
Outputs:
- factors: float32 [8192, 256], P(('grp', 'pts'))
The draws below stay inside these ranges and needn't reach their ends.
All inputs are finite; a program needn't handle non-finite values. Where the reference program divides by a largest or mean magnitude, that divisor is 1e-20 or more.
Results may differ from the reference program's by a relative error of at most 0.0003.
Values sent between devices are 32-bit elements; how exact they have to be, the bound alone decides.
No kernel may reach another device: no remote copies, remote signals or barrier semaphores. Data moves between devices by JAX's collectives and lax.ppermute only.
A program may use at most 64 MiB of HBM per device.

```python
import math
import jax
import jax.numpy as jnp
from jax import lax

D = 2048
RANK = 256
ITERS = 2
ALL = 8192
NS = 6144
NT = 2048


def shared_latent(key):
    latent_width = 2 * RANK
    latent = jax.random.normal(jax.random.fold_in(key, 701), (ALL, latent_width), jnp.float32)
    anchors = jax.random.normal(jax.random.fold_in(key, 702), (RANK, latent_width), jnp.float32)
    return (latent, anchors)


def draw_points(key, part):
    latent, anchors = shared_latent(key)
    latent_width = latent.shape[1]
    latent_basis = jax.random.normal(jax.random.fold_in(key, 703), (latent_width, D), jnp.float32) / math.sqrt(D)
    shaped = jnp.dot(latent, latent_basis) / math.sqrt(latent_width)
    noise_part = jax.random.normal(jax.random.fold_in(key, 704), (ALL, D), jnp.float32)
    scales = jnp.exp(jax.random.uniform(jax.random.fold_in(key, 705), (ALL, 1), jnp.float32, math.log(0.4), math.log(4.0)))
    values = shaped + 0.5 * noise_part / math.sqrt(D)
    return jnp.clip(scales * values, -2.0, 2.0)


def draw_log_factor(key, part):
    latent, anchors = shared_latent(key)
    latent_width = latent.shape[1]
    aligned = 2.0 * jnp.dot(latent, anchors.T) / math.sqrt(latent_width)
    rough_part = jax.random.normal(jax.random.fold_in(key, 711), (ALL, RANK), jnp.float32)
    values = aligned + rough_part
    return jnp.clip(values, -40.0, 320.0)


def draw_masses(key, part):
    position = jnp.arange(ALL).astype(jnp.float32)
    within = jnp.where(position < NS, position / NS, (position - NS) / NT)
    lower_end = math.log(0.5)
    upper_end = math.log(2.0)
    rough_factor = jnp.exp(jax.random.uniform(jax.random.fold_in(key, 721), (ALL,), jnp.float32, lower_end, upper_end))
    return (1.0 + 2.0 * within) * rough_factor


def setup_inputs(seed: int = 0) -> dict:
    splits = jax.random.split(jax.random.key(seed), 4)
    points = draw_points(jax.random.fold_in(splits[3], 71), 0)
    log_factor = draw_log_factor(jax.random.fold_in(splits[3], 71), 0)
    masses = draw_masses(jax.random.fold_in(splits[3], 71), 0)
    return {"points": points, "log_factor": log_factor, "masses": masses}


step_scale = 4.0
highest = lax.Precision.HIGHEST


def side_sums(side_points, side_scaled):
    column_sums = jnp.sum(side_scaled, axis=0)
    mass_total = jnp.sum(column_sums)
    moment = lax.dot_general(side_points, side_scaled, (((0,), (0,)), ((), ())), precision=highest, preferred_element_type=jnp.float32) / mass_total
    squares = jnp.sum(side_points * side_points, axis=1)
    norm_moment = jnp.dot(squares, side_scaled, precision=highest, preferred_element_type=jnp.float32) / mass_total
    return column_sums / mass_total, moment, norm_moment


def cost_gradient(side_points, column_share, moment, norm_moment, marginal):
    squares = jnp.sum(side_points * side_points, axis=1)
    cross_term = jnp.dot(side_points, moment, precision=highest, preferred_element_type=jnp.float32)
    return (squares[:, None] * column_share[None, :] - 2.0 * cross_term + norm_moment[None, :]) / marginal[None, :]


def reference(points, log_factor, masses):
    source_points = points[:NS]
    target_points = points[NS:]
    for iteration in range(ITERS):
        weights = jax.nn.softmax(log_factor, axis=1)
        scaled = weights * masses[:, None]
        source_share, source_moment, source_norms = side_sums(source_points, scaled[:NS])
        target_share, target_moment, target_norms = side_sums(target_points, scaled[NS:])
        marginal = 0.5 * (source_share + target_share)
        source_gradient = cost_gradient(source_points, target_share, target_moment, target_norms, marginal)
        target_gradient = cost_gradient(target_points, source_share, source_moment, source_norms, marginal)
        gradient = jnp.concatenate([source_gradient, target_gradient], axis=0)
        centred = gradient - jnp.mean(gradient, axis=1, keepdims=True)
        step_rate = step_scale / (jnp.max(jnp.abs(centred)) + 1e-6)
        log_factor = log_factor - step_rate * gradient
    return RANK * jax.nn.softmax(log_factor, axis=1)
```

```python
import jax
import jax.numpy as jnp
from jax import lax
from jax.sharding import Mesh, PartitionSpec as P

ITERS = 2

step_scale = 4.0
highest = lax.Precision.HIGHEST
AXES = ("side", "core", "hi", "lo")
SWAP = [(0, 1), (1, 0)]
PAD = 8


def swap(value, axis):
    return lax.ppermute(value, axis, SWAP)


def exchange(blocks):
    return lax.all_to_all(blocks, "hi", 0, 0, tiled=True)


def gather_hi(block, hi):
    return exchange(jnp.broadcast_to(block[None], (hi,) + block.shape))


def contract_rows(left, right):
    return lax.dot_general(
        left,
        right,
        (((0,), (0,)), ((), ())),
        precision=highest,
        preferred_element_type=jnp.float32,
    )


def times(left, right):
    return jnp.dot(left, right, precision=highest, preferred_element_type=jnp.float32)


def to_side(own):
    half = own.shape[0] // 2
    group = 2 * lax.axis_index("side") + lax.axis_index("core")
    first = lax.ppermute(own[:half], ("side", "core"), [(2, 0), (3, 2)])
    second = lax.ppermute(own[half:], ("side", "core"), [(2, 1)])
    kept = jnp.where(group == 3, own[half:], jnp.zeros_like(second))
    return jnp.where(group == 1, second, jnp.where(group == 3, kept, first))


def from_side(base, extra):
    group = 2 * lax.axis_index("side") + lax.axis_index("core")
    half = extra.shape[0]
    first = lax.ppermute(extra, ("side", "core"), [(0, 2), (2, 3)])
    second = lax.ppermute(extra, ("side", "core"), [(1, 2)])
    top = jnp.where(group < 2, base[:half], first)
    bottom = jnp.where(group < 2, base[half:], jnp.where(group == 2, second, extra))
    return jnp.concatenate([top, bottom], axis=0)


def make_body(hi):
    lo = 2

    def reduce_moment(held, statistics, low):
        feats, rank = held.shape
        chunk = feats // (lo * hi)
        ra = max(8, (2 * chunk // 3 + 4) // 8 * 8)
        rb = chunk - ra
        held = held.reshape(lo, feats // lo, rank)
        part_a, part_b = held[:, : hi * ra], held[:, hi * ra :]
        keep_a = jnp.where(low, part_a[1], part_a[0])
        send_a = jnp.where(low, part_a[0], part_a[1])
        got_a = swap(jnp.concatenate([send_a, statistics], axis=0), "lo")
        blocks = part_b.reshape(lo, hi, rb, rank).transpose(1, 0, 2, 3)
        sum_b = jnp.sum(exchange(blocks), axis=0)
        keep_b = jnp.where(low, sum_b[1], sum_b[0])
        got_b = swap(jnp.where(low, sum_b[0], sum_b[1]), "lo")
        statistics = statistics + got_a[hi * ra :]
        blocks = jnp.concatenate(
            [
                (keep_a + got_a[: hi * ra]).reshape(hi, ra, rank),
                jnp.broadcast_to(statistics[None], (hi, PAD, rank)),
            ],
            axis=1,
        )
        sum_a = jnp.sum(exchange(blocks), axis=0)
        mine = jnp.concatenate([sum_a, keep_b + got_b], axis=0)
        facing = swap(mine, "side")
        return sum_a[ra:], facing[ra : ra + PAD], facing[:ra], facing[ra + PAD :]

    def gather_moment(chunk_a, chunk_b, low):
        ra, rank = chunk_a.shape
        rb = chunk_b.shape[0]
        got_b = swap(chunk_b, "lo")
        pair_b = jnp.stack([jnp.where(low, got_b, chunk_b), jnp.where(low, chunk_b, got_b)])
        mine_a = gather_hi(chunk_a, hi).reshape(hi * ra, rank)
        got_a = swap(mine_a, "lo")
        all_b = gather_hi(pair_b, hi)
        pieces = []
        for bit in range(lo):
            pieces.append(jnp.where(low == (bit == 1), mine_a, got_a))
            pieces.append(all_b[:, bit].reshape(hi * rb, rank))
        return jnp.concatenate(pieces, axis=0)

    def body(points, log_factor, masses):
        source = lax.axis_index("side") == 0
        core = lax.axis_index("core") == 1
        low = lax.axis_index("lo") == 1
        rows, width = points.shape
        rank = log_factor.shape[1]
        half = width // 2
        devices = 1
        for axis in AXES:
            devices *= lax.axis_size(axis)

        extra = to_side(points)
        base = jnp.where(source, points, 0.0)
        whole = jnp.concatenate([base, extra], axis=0)
        near = jnp.where(core, whole[:, half:], whole[:, :half])
        far = jnp.where(core, whole[:, :half], whole[:, half:])
        logits = jnp.concatenate([log_factor, to_side(log_factor)], axis=0)
        mass = masses[:, None]
        mass = jnp.concatenate([jnp.where(source, mass, 0.0), to_side(mass)], axis=0)
        squares = jnp.sum(near * near, axis=1, keepdims=True) + jnp.sum(
            far * far, axis=1, keepdims=True
        )
        real = source | (lax.broadcasted_iota(jnp.int32, (logits.shape[0], 1), 0) >= rows)

        for iteration in range(ITERS):
            scaled = jax.nn.softmax(logits, axis=1) * mass
            statistics = jnp.concatenate(
                [
                    jnp.sum(scaled * squares, axis=0, keepdims=True),
                    jnp.sum(scaled, axis=0, keepdims=True),
                    jnp.zeros((PAD - 2, rank), jnp.float32),
                ],
                axis=0,
            )
            statistics = statistics + swap(statistics, "core")
            other = swap(contract_rows(far, scaled), "core")
            held = contract_rows(near, scaled) + other
            own, facing, chunk_a, chunk_b = reduce_moment(held, statistics, low)
            moment = gather_moment(chunk_a, chunk_b, low)
            other = swap(moment, "core")
            cross = times(near, moment) + times(far, other)
            own_mass = jnp.sum(own[1])
            mass_total = jnp.sum(facing[1])
            share = facing[1] / mass_total
            marginal = 0.5 * (own[1] / own_mass + share)
            gradient = (
                squares * share[None, :]
                - 2.0 * (cross / mass_total)
                + (facing[0] / mass_total)[None, :]
            ) / marginal[None, :]
            centred = gradient - jnp.mean(gradient, axis=1, keepdims=True)
            largest = jnp.max(jnp.where(real, jnp.abs(centred), 0.0))
            spread = jnp.full((devices, 128), largest, jnp.float32)
            largest = jnp.max(lax.all_to_all(spread, AXES, 0, 0, tiled=True))
            logits = logits - step_scale / (largest + 1e-06) * gradient
        factors = rank * jax.nn.softmax(logits, axis=1)
        return from_side(factors[:rows], factors[rows:])

    return body


def solution(mesh):
    pts = mesh.shape["pts"]
    hi = pts // 2
    split = Mesh(mesh.devices.reshape(2, 2, hi, 2), AXES)
    in_specs = (P(AXES, None), P(AXES, None), P(AXES))
    return jax.shard_map(
        make_body(hi), mesh=split, in_specs=in_specs, out_specs=P(AXES, None), check_vma=False
    )
```

```python
import jax
import jax.numpy as jnp
from jax import lax
from jax.experimental import pallas as pl
from jax.experimental.pallas import tpu as pltpu
from jax.sharding import Mesh, PartitionSpec as P

ITERS = 2

step_scale = 4.0
highest = lax.Precision.HIGHEST
PAD = 8


def swap(value, axis):
    return lax.ppermute(value, axis, [(0, 1), (1, 0)])


def together(*values):
    return lax.optimization_barrier(values)


def contract_rows(left, right):
    return lax.dot_general(
        left,
        right,
        (((0,), (0,)), ((), ())),
        precision=highest,
        preferred_element_type=jnp.float32,
    )


def times(left, right):
    return jnp.dot(left, right, precision=highest, preferred_element_type=jnp.float32)


def pick_kernel(order_ref, in_ref, out_ref):
    out_ref[...] = in_ref[...]


def pick_blocks(array, order, count):
    rows, columns = array.shape
    width = columns // count
    if width % 128:
        return array.reshape(rows, count, width)[:, order].reshape(rows, -1)
    picked = order.shape[0]
    return pl.pallas_call(
        pick_kernel,
        grid_spec=pltpu.PrefetchScalarGridSpec(
            num_scalar_prefetch=1,
            grid=(picked,),
            in_specs=[pl.BlockSpec((rows, width), lambda i, order: (0, order[i]))],
            out_specs=pl.BlockSpec((rows, width), lambda i, order: (0, i)),
        ),
        out_shape=jax.ShapeDtypeStruct((rows, picked * width), array.dtype),
        name="pick_blocks",
    )(order, array)


def to_side(own):
    half = own.shape[0] // 2
    group = 2 * lax.axis_index("side") + lax.axis_index("core")
    first = lax.ppermute(own[:half], ("side", "core"), [(2, 0), (3, 2)])
    second = lax.ppermute(own[half:], ("side", "core"), [(2, 1)])
    kept = jnp.where(group == 3, own[half:], jnp.zeros_like(second))
    return jnp.where(group == 1, second, jnp.where(group == 3, kept, first))


def from_side(base, extra):
    group = 2 * lax.axis_index("side") + lax.axis_index("core")
    half = extra.shape[0]
    first = lax.ppermute(extra, ("side", "core"), [(0, 2), (2, 3)])
    second = lax.ppermute(extra, ("side", "core"), [(1, 2)])
    top = jnp.where(group < 2, base[:half], first)
    bottom = jnp.where(group < 2, base[half:], jnp.where(group == 2, second, extra))
    return jnp.concatenate([top, bottom], axis=0)


def outer_halves(value):
    half = value.shape[0] // 2
    return value[:half], value[half:]


def inner_halves(value):
    rows, columns = value.shape
    value = value.reshape(2, 2, rows // 4, columns)
    return value[:, 0].reshape(-1, columns), value[:, 1].reshape(-1, columns)


def join_inner(mine, got):
    rows, columns = mine.shape
    blocks = [v.reshape(2, 1, rows // 2, columns) for v in (mine, got)]
    return jnp.concatenate(blocks, axis=1).reshape(2 * rows, columns)


def across(value, axis, flip):
    pairs = [(i, (i ^ 2) ^ flip) for i in range(4)]
    return lax.ppermute(value, ("side", axis), pairs)


def reduce_moment(held, statistics, bits):
    half = held.shape[1] // 2
    parts = [held[:, :half], held[:, half:]]
    stats = [statistics[:, :half], statistics[:, half:]]
    for stage in range(len(bits) - 1):
        axes = [bits[stage]] * 2
        if stage < 2:
            axes = [bits[stage], bits[1 - stage]]
        kept, sent = [None, None], [None, None]
        for i in range(2):
            inner = i == 1 and stage == 0
            kept[i], sent[i] = (inner_halves if inner else outer_halves)(parts[i])
            sent[i] = jnp.concatenate([sent[i], stats[i]], axis=0)
        sent = together(*sent)
        got = together(*(swap(sent[i], axes[i]) for i in range(2)))
        for i in range(2):
            rows = kept[i].shape[0]
            parts[i] = kept[i] + got[i][:rows]
            stats[i] = stats[i] + got[i][rows:]
    kept, sent = outer_halves(jnp.concatenate(parts, axis=1))
    statistics = jnp.concatenate(stats, axis=1)
    last = bits[-1]
    messages = together(
        jnp.concatenate([kept, statistics], axis=0),
        jnp.concatenate([sent, statistics], axis=0),
    )
    straight, crossed, peer = together(
        across(messages[0], last, 0), across(messages[1], last, 1), swap(statistics, last)
    )
    rows = kept.shape[0]
    facing = straight + crossed
    return statistics + peer, facing[rows:], facing[:rows]


def gather_moment(chunk, bits):
    value = jnp.concatenate([chunk, swap(chunk, bits[-1])], axis=0)
    half = value.shape[1] // 2
    parts = [value[:, :half], value[:, half:]]
    for stage in reversed(range(len(bits) - 1)):
        axes = [bits[stage]] * 2
        if stage < 2:
            axes = [bits[stage], bits[1 - stage]]
        parts = together(*parts)
        got = together(*(swap(parts[i], axes[i]) for i in range(2)))
        joined = []
        for i in range(2):
            if i == 1 and stage == 0:
                joined.append(join_inner(parts[i], got[i]))
            else:
                joined.append(jnp.concatenate([parts[i], got[i]], axis=0))
        parts = joined
    return jnp.concatenate(parts, axis=1)


def make_body(axes):
    bits = axes[2:][::-1]

    def body(points, log_factor, masses):
        source = lax.axis_index("side") == 0
        rows, width = points.shape
        rank = log_factor.shape[1]
        devices, place = 1, lax.axis_index("core")
        for axis in axes:
            devices *= lax.axis_size(axis)
        for axis in bits:
            place = 2 * place + lax.axis_index(axis)
        blocks = devices // 2
        order = jnp.arange(blocks, dtype=jnp.int32) ^ place.astype(jnp.int32)

        extra = to_side(points)
        halves = order[: blocks // 2], order[blocks // 2 :]
        near, far = (
            jnp.concatenate([pick_blocks(v, half, blocks) for v in (points, extra)], axis=0)
            for half in halves
        )
        logits = jnp.concatenate([log_factor, to_side(log_factor)], axis=0)
        mass = masses[:, None]
        mass = jnp.concatenate([jnp.where(source, mass, 0.0), to_side(mass)], axis=0)
        squares = jnp.concatenate(
            [jnp.sum(v * v, axis=1, keepdims=True) for v in (points, extra)], axis=0
        )
        real = source | (lax.broadcasted_iota(jnp.int32, (logits.shape[0], 1), 0) >= rows)

        for iteration in range(ITERS):
            scaled = jax.nn.softmax(logits, axis=1) * mass
            columns = jnp.sum(scaled, axis=0, keepdims=True)
            statistics = jnp.concatenate(
                [
                    jnp.sum(scaled * squares, axis=0, keepdims=True),
                    columns,
                    jnp.broadcast_to(jnp.sum(columns, axis=1, keepdims=True), columns.shape),
                    jnp.zeros((PAD - 3, rank), jnp.float32),
                ],
                axis=0,
            )
            statistics = statistics + swap(statistics, "core")
            other = swap(contract_rows(far, scaled), "core")
            held = contract_rows(near, scaled) + other
            own, facing, chunk = reduce_moment(held, statistics, bits)
            moment = gather_moment(chunk, bits)
            other = swap(moment, "core")
            cross = times(near, moment) + times(far, other)
            share = facing[1:2] / facing[2:3]
            marginal = 0.5 * (own[1:2] / own[2:3] + share)
            gradient = (
                squares * share - 2.0 * (cross / facing[2:3]) + facing[0:1] / facing[2:3]
            ) / marginal
            centred = gradient - jnp.mean(gradient, axis=1, keepdims=True)
            largest = jnp.max(jnp.where(real, jnp.abs(centred), 0.0))
            spread = jnp.full((devices, 128), largest, jnp.float32)
            largest = jnp.max(lax.all_to_all(spread, axes, 0, 0, tiled=True))
            logits = logits - step_scale / (largest + 1e-06) * gradient
        factors = rank * jax.nn.softmax(logits, axis=1)
        return from_side(factors[:rows], factors[rows:])

    return body


def solution(mesh):
    pts = mesh.shape["pts"]
    count = pts.bit_length() - 1
    axes = ("side", "core") + tuple(f"bit{i}" for i in reversed(range(count)))
    split = Mesh(mesh.devices.reshape((2,) * len(axes)), axes)
    in_specs = (P(axes, None), P(axes, None), P(axes))
    return jax.shard_map(
        make_body(axes), mesh=split, in_specs=in_specs, out_specs=P(axes, None), check_vma=False
    )
```

```python
import functools

import jax
import jax.numpy as jnp
from jax import lax
from jax.experimental import pallas as pl
from jax.experimental.pallas import tpu as pltpu
from jax.sharding import Mesh, PartitionSpec as P

ITERS = 2

step_scale = 4.0
highest = lax.Precision.HIGHEST
PAD = 8


def swap(value, axis):
    return lax.ppermute(value, axis, [(0, 1), (1, 0)])


def together(*values):
    return lax.optimization_barrier(values)


def contract_rows(left, right):
    return lax.dot_general(
        left,
        right,
        (((0,), (0,)), ((), ())),
        precision=highest,
        preferred_element_type=jnp.float32,
    )


def times(left, right):
    return jnp.dot(left, right, precision=highest, preferred_element_type=jnp.float32)


def own_place(bits):
    place = lax.axis_index("core")
    for axis in bits:
        place = 2 * place + lax.axis_index(axis)
    return place


def column_copies(source, begin, parts, place, sems):
    count = sems.shape[0]
    width = source.shape[1] // count
    rows = parts[0].shape[0]
    copies = []
    for i in range(count):
        column = pl.multiple_of((i ^ place) * width, width)
        copies.append(
            pltpu.make_async_copy(
                source.at[pl.ds(begin, rows), pl.ds(column, width)],
                parts[2 * i // count].at[:, pl.ds(i % (count // 2) * width, width)],
                sems.at[i],
            )
        )
    return copies


def put_rows(parts, targets, top, sems):
    rows = parts[0].shape[0]
    copies = [
        pltpu.make_async_copy(parts[i], targets[i].at[pl.ds(top, rows), :], sems.at[i])
        for i in range(2)
    ]
    for copy in copies:
        copy.start()
    for copy in copies:
        copy.wait()


def base_kernel(bits, points, near, far, near_part, far_part, sems, out_sems):
    parts = near_part, far_part
    copies = column_copies(points, 0, parts, own_place(bits), sems)
    for copy in copies:
        copy.start()
    for copy in copies:
        copy.wait()
    put_rows(parts, (near, far), 0, out_sems)


def extra_kernel(
    bits, points, first, second, near_in, far_in, near, far, near_part, far_part, sems, out_sems
):
    del near_in, far_in
    parts = near_part, far_part
    place = own_place(bits)
    group = 2 * lax.axis_index("side") + lax.axis_index("core")
    half = first.shape[0]

    @pl.when((group == 0) | (group == 2))
    def _():
        for copy in column_copies(first, 0, parts, place, sems):
            copy.start()

    @pl.when(group == 1)
    def _():
        for copy in column_copies(second, 0, parts, place, sems):
            copy.start()

    @pl.when(group == 3)
    def _():
        for copy in column_copies(points, half, parts, place, sems):
            copy.start()

    for copy in column_copies(first, 0, parts, place, sems):
        copy.wait()
    put_rows(parts, (near, far), points.shape[0], out_sems)


def arrange(points, first, second, bits):
    rows, width = points.shape
    blocks = 2 ** (1 + len(bits))
    half = rows // 2
    if (width // blocks) % 128:
        group = 2 * lax.axis_index("side") + lax.axis_index("core")
        extra = jnp.where(group == 1, second, jnp.where(group == 3, points[half:], first))
        whole = jnp.concatenate([points, extra], axis=0)
        order = jnp.arange(blocks) ^ own_place(bits)
        whole = whole.reshape(rows + half, blocks, -1)[:, order].reshape(rows + half, width)
        return whole[:, : width // 2], whole[:, width // 2 :]
    anywhere = pl.BlockSpec(memory_space=pl.ANY)
    shape = jax.ShapeDtypeStruct((rows + half, width // 2), points.dtype)

    def call(kernel, count, inputs, name, aliases):
        return pl.pallas_call(
            functools.partial(kernel, bits),
            out_shape=(shape, shape),
            in_specs=[anywhere] * inputs,
            out_specs=(anywhere, anywhere),
            scratch_shapes=[
                pltpu.VMEM((count, width // 2), points.dtype),
                pltpu.VMEM((count, width // 2), points.dtype),
                pltpu.SemaphoreType.DMA((blocks,)),
                pltpu.SemaphoreType.DMA((2,)),
            ],
            input_output_aliases=aliases,
            name=name,
        )

    near, far = call(base_kernel, rows, 1, "base_rows", {})(points)
    return call(extra_kernel, half, 5, "extra_rows", {3: 0, 4: 1})(
        points, first, second, near, far
    )


def move(own):
    half = own.shape[0] // 2
    own, head = together(own, own[:half])
    first = lax.ppermute(head, ("side", "core"), [(2, 0), (3, 2)])
    second = lax.ppermute(own[half:], ("side", "core"), [(2, 1)])
    return first, second


def from_side(base, extra):
    group = 2 * lax.axis_index("side") + lax.axis_index("core")
    half = extra.shape[0]
    first = lax.ppermute(extra, ("side", "core"), [(0, 2), (2, 3)])
    second = lax.ppermute(extra, ("side", "core"), [(1, 2)])
    top = jnp.where(group < 2, base[:half], first)
    bottom = jnp.where(group < 2, base[half:], jnp.where(group == 2, second, extra))
    return jnp.concatenate([top, bottom], axis=0)


def outer_halves(value):
    half = value.shape[0] // 2
    return value[:half], value[half:]


def inner_halves(value):
    rows, columns = value.shape
    value = value.reshape(2, 2, rows // 4, columns)
    return value[:, 0].reshape(-1, columns), value[:, 1].reshape(-1, columns)


def join_inner(mine, got):
    rows, columns = mine.shape
    blocks = [v.reshape(2, 1, rows // 2, columns) for v in (mine, got)]
    return jnp.concatenate(blocks, axis=1).reshape(2 * rows, columns)


def across(value, axis, flip):
    pairs = [(i, (i ^ 2) ^ flip) for i in range(4)]
    return lax.ppermute(value, ("side", axis), pairs)


def reduce_moment(held, statistics, bits):
    half = held.shape[1] // 2
    parts = [held[:, :half], held[:, half:]]
    stats = [statistics[:, :half], statistics[:, half:]]
    for stage in range(len(bits) - 1):
        axes = [bits[stage]] * 2
        if stage < 2:
            axes = [bits[stage], bits[1 - stage]]
        kept, sent = [None, None], [None, None]
        for i in range(2):
            inner = i == 1 and stage == 0
            kept[i], sent[i] = (inner_halves if inner else outer_halves)(parts[i])
            sent[i] = jnp.concatenate([sent[i], stats[i]], axis=0)
        sent = together(*sent)
        got = together(*(swap(sent[i], axes[i]) for i in range(2)))
        for i in range(2):
            rows = kept[i].shape[0]
            parts[i] = kept[i] + got[i][:rows]
            stats[i] = stats[i] + got[i][rows:]
    kept, sent = outer_halves(jnp.concatenate(parts, axis=1))
    statistics = jnp.concatenate(stats, axis=1)
    last = bits[-1]
    messages = together(
        jnp.concatenate([kept, statistics], axis=0),
        jnp.concatenate([sent, statistics], axis=0),
    )
    straight, crossed = together(across(messages[0], last, 0), across(messages[1], last, 1))
    return statistics, straight + crossed


def gather_moment(own, facing, bits):
    rows = facing.shape[0] - PAD
    chunk, facing = facing[:rows], facing[rows:]
    got = swap(jnp.concatenate([chunk, own], axis=0), bits[-1])
    both = jnp.concatenate([own + got[rows:], facing], axis=0)
    value = jnp.concatenate([chunk, got[:rows]], axis=0)
    half = value.shape[1] // 2
    parts = [value[:, :half], value[:, half:]]
    for stage in reversed(range(len(bits) - 1)):
        axes = [bits[stage]] * 2
        if stage < 2:
            axes = [bits[stage], bits[1 - stage]]
        if stage == 0:
            *parts, both = together(*parts, both)
            *got, peer = together(
                *(swap(parts[i], axes[i]) for i in range(2)), swap(both, "core")
            )
        else:
            parts = together(*parts)
            got = together(*(swap(parts[i], axes[i]) for i in range(2)))
        joined = []
        for i in range(2):
            if i == 1 and stage == 0:
                joined.append(join_inner(parts[i], got[i]))
            else:
                joined.append(jnp.concatenate([parts[i], got[i]], axis=0))
        parts = joined
    both = both + peer
    return jnp.concatenate(parts, axis=1), both[:PAD], both[PAD:]


def make_body(axes):
    bits = axes[2:][::-1]

    def body(points, log_factor, masses):
        source = lax.axis_index("side") == 0
        group = 2 * lax.axis_index("side") + lax.axis_index("core")
        rows, width = points.shape
        rank = log_factor.shape[1]
        half = rows // 2
        devices = 1
        for axis in axes:
            devices *= lax.axis_size(axis)

        moved = move(points)
        squares = jnp.sum(points * points, axis=1, keepdims=True)
        mass = masses[:, None]
        lanes = lax.broadcasted_iota(jnp.int32, (rows, 128), 1)
        packed = jnp.concatenate(
            [log_factor, jnp.where(lanes < 64, mass, squares)], axis=1
        )
        first, second = move(packed)
        extra = jnp.where(group == 1, second, jnp.where(group == 3, packed[half:], first))
        near, far = arrange(points, *moved, bits)
        logits = jnp.concatenate([log_factor, extra[:, :rank]], axis=0)
        mass = jnp.concatenate(
            [jnp.where(source, mass, 0.0), extra[:, rank : rank + 1]], axis=0
        )
        squares = jnp.concatenate([squares, extra[:, rank + 64 : rank + 65]], axis=0)
        real = source | (lax.broadcasted_iota(jnp.int32, (logits.shape[0], 1), 0) >= rows)

        for iteration in range(ITERS):
            scaled = jax.nn.softmax(logits, axis=1) * mass
            columns = jnp.sum(scaled, axis=0, keepdims=True)
            statistics = jnp.concatenate(
                [
                    jnp.sum(scaled * squares, axis=0, keepdims=True),
                    columns,
                    jnp.broadcast_to(jnp.sum(columns, axis=1, keepdims=True), columns.shape),
                    jnp.zeros((PAD - 3, rank), jnp.float32),
                ],
                axis=0,
            )
            other = swap(contract_rows(far, scaled), "core")
            held, other = together(contract_rows(near, scaled), other)
            own, facing = reduce_moment(held + other, statistics, bits)
            moment, own, facing = gather_moment(own, facing, bits)
            cross, other = together(times(near, moment), swap(moment, "core"))
            cross = cross + times(far, other)
            share = facing[1:2] / facing[2:3]
            marginal = 0.5 * (own[1:2] / own[2:3] + share)
            gradient = (
                squares * share - 2.0 * (cross / facing[2:3]) + facing[0:1] / facing[2:3]
            ) / marginal
            centred = gradient - jnp.mean(gradient, axis=1, keepdims=True)
            largest = jnp.max(jnp.where(real, jnp.abs(centred), 0.0))
            spread = jnp.full((devices, 128), largest, jnp.float32)
            largest = jnp.max(lax.all_to_all(spread, axes, 0, 0, tiled=True))
            logits = logits - step_scale / (largest + 1e-06) * gradient
        factors = rank * jax.nn.softmax(logits, axis=1)
        return from_side(factors[:rows], factors[rows:])

    return body


def solution(mesh):
    pts = mesh.shape["pts"]
    count = pts.bit_length() - 1
    axes = ("side", "core") + tuple(f"bit{i}" for i in reversed(range(count)))
    split = Mesh(mesh.devices.reshape((2,) * len(axes)), axes)
    in_specs = (P(axes, None), P(axes, None), P(axes))
    return jax.shard_map(
        make_body(axes), mesh=split, in_specs=in_specs, out_specs=P(axes, None), check_vma=False
    )
```

```python
import functools

import jax
import jax.numpy as jnp
from jax import lax
from jax.experimental import pallas as pl
from jax.experimental.pallas import tpu as pltpu
from jax.sharding import Mesh, PartitionSpec as P


ITERS = 2

step_scale = 4.0
highest = lax.Precision.HIGHEST
PAD = 8


def swap(value, axis):
    return lax.ppermute(value, axis, [(0, 1), (1, 0)])


def together(*values):
    return lax.optimization_barrier(values)


def contract_rows(left, right):
    return lax.dot_general(
        left,
        right,
        (((0,), (0,)), ((), ())),
        precision=highest,
        preferred_element_type=jnp.float32,
    )


def times(left, right):
    return jnp.dot(left, right, precision=highest, preferred_element_type=jnp.float32)


def own_place(bits):
    place = lax.axis_index("core")
    for axis in bits:
        place = 2 * place + lax.axis_index(axis)
    return place


def column_copies(source, begin, parts, place, sems):
    count = sems.shape[0]
    width = source.shape[1] // count
    rows = parts[0].shape[0]
    copies = []
    for i in range(count):
        column = pl.multiple_of((i ^ place) * width, width)
        copies.append(
            pltpu.make_async_copy(
                source.at[pl.ds(begin, rows), pl.ds(column, width)],
                parts[2 * i // count].at[:, pl.ds(i % (count // 2) * width, width)],
                sems.at[i],
            )
        )
    return copies


def put_rows(parts, targets, top, sems):
    rows = parts[0].shape[0]
    copies = [
        pltpu.make_async_copy(parts[i], targets[i].at[pl.ds(top, rows), :], sems.at[i])
        for i in range(2)
    ]
    for copy in copies:
        copy.start()
    for copy in copies:
        copy.wait()


def base_kernel(bits, points, near, far, near_part, far_part, sems, out_sems):
    parts = near_part, far_part
    copies = column_copies(points, 0, parts, own_place(bits), sems)
    for copy in copies:
        copy.start()
    for copy in copies:
        copy.wait()
    put_rows(parts, (near, far), 0, out_sems)


def extra_kernel(
    bits, points, first, second, near_in, far_in, near, far, near_part, far_part, sems, out_sems
):
    del near_in, far_in
    parts = near_part, far_part
    place = own_place(bits)
    group = 2 * lax.axis_index("side") + lax.axis_index("core")
    half = first.shape[0]

    @pl.when((group == 0) | (group == 2))
    def _():
        for copy in column_copies(first, 0, parts, place, sems):
            copy.start()

    @pl.when(group == 1)
    def _():
        for copy in column_copies(second, 0, parts, place, sems):
            copy.start()

    @pl.when(group == 3)
    def _():
        for copy in column_copies(points, half, parts, place, sems):
            copy.start()

    for copy in column_copies(first, 0, parts, place, sems):
        copy.wait()
    put_rows(parts, (near, far), points.shape[0], out_sems)


def arrange_base(points, bits):
    rows, width = points.shape
    blocks = 2 ** (1 + len(bits))
    if (width // blocks) % 128:
        order = jnp.arange(blocks) ^ own_place(bits)
        whole = points.reshape(rows, blocks, -1)[:, order].reshape(rows, width)
        return whole[:, : width // 2], whole[:, width // 2 :]
    return arrange_call(base_kernel, points, rows, bits, {})(points)


def arrange_extra(points, first, second, near, far, bits):
    rows, width = points.shape
    blocks = 2 ** (1 + len(bits))
    half = rows // 2
    if (width // blocks) % 128:
        group = 2 * lax.axis_index("side") + lax.axis_index("core")
        extra = jnp.where(group == 1, second, jnp.where(group == 3, points[half:], first))
        extra = arrange_base(extra, bits)
        return tuple(jnp.concatenate(pair, axis=0) for pair in zip((near, far), extra))
    return arrange_call(extra_kernel, points, half, bits, {3: 0, 4: 1})(
        points, first, second, near, far
    )


def arrange_call(kernel, points, count, bits, aliases):
    rows, width = points.shape
    anywhere = pl.BlockSpec(memory_space=pl.ANY)
    shape = jax.ShapeDtypeStruct((rows + rows // 2, width // 2), points.dtype)
    part = pltpu.VMEM((count, width // 2), points.dtype)
    return pl.pallas_call(
        functools.partial(kernel, bits),
        out_shape=(shape, shape),
        in_specs=[anywhere] * (5 if aliases else 1),
        out_specs=(anywhere, anywhere),
        scratch_shapes=[
            part,
            part,
            pltpu.SemaphoreType.DMA((2 ** (1 + len(bits)),)),
            pltpu.SemaphoreType.DMA((2,)),
        ],
        input_output_aliases=aliases,
    )


def move(own):
    half = own.shape[0] // 2
    own, head = together(own, own[:half])
    first = lax.ppermute(head, ("side", "core"), [(2, 0), (3, 2)])
    second = lax.ppermute(own[half:], ("side", "core"), [(2, 1)])
    return first, second


def from_side(base, extra):
    group = 2 * lax.axis_index("side") + lax.axis_index("core")
    half = extra.shape[0]
    first = lax.ppermute(extra, ("side", "core"), [(0, 2), (2, 3)])
    second = lax.ppermute(extra, ("side", "core"), [(1, 2)])
    top = jnp.where(group < 2, base[:half], first)
    bottom = jnp.where(group < 2, base[half:], jnp.where(group == 2, second, extra))
    return jnp.concatenate([top, bottom], axis=0)


def outer_halves(value):
    half = value.shape[0] // 2
    return value[:half], value[half:]


def inner_halves(value):
    rows, columns = value.shape
    value = value.reshape(2, 2, rows // 4, columns)
    return value[:, 0].reshape(-1, columns), value[:, 1].reshape(-1, columns)


def join_inner(mine, got):
    rows, columns = mine.shape
    blocks = [v.reshape(2, 1, rows // 2, columns) for v in (mine, got)]
    return jnp.concatenate(blocks, axis=1).reshape(2 * rows, columns)


def across(value, axis, flip):
    pairs = [(i, (i ^ 2) ^ flip) for i in range(4)]
    return lax.ppermute(value, ("side", axis), pairs)


def stage_axes(bits, stage):
    if stage < 2:
        return bits[stage], bits[1 - stage]
    return bits[stage], bits[stage]


def halve(parts, stats, bits):
    parts, stats = list(parts), list(stats)
    for stage in range(len(bits) - 1):
        axes = stage_axes(bits, stage)
        kept, sent = [None, None], [None, None]
        for i in range(2):
            inner = i == 1 and stage == 0
            kept[i], sent[i] = (inner_halves if inner else outer_halves)(parts[i])
            sent[i] = jnp.concatenate([sent[i], stats[i]], axis=0)
        sent = together(*sent)
        got = [swap(sent[i], axes[i]) for i in range(2)]
        got = together(*got)
        for i in range(2):
            rows = kept[i].shape[0]
            parts[i] = kept[i] + got[i][:rows]
            stats[i] = stats[i] + got[i][rows:]
    return parts, stats


def last_messages(part, stats):
    kept, sent = outer_halves(part)
    return jnp.concatenate([kept, stats], axis=0), jnp.concatenate([sent, stats], axis=0)


def reduce_moment(held, statistics, bits):
    half = held.shape[1] // 2
    parts, stats = halve(
        (held[:, :half], held[:, half:]),
        (statistics[:, :half], statistics[:, half:]),
        bits,
    )
    statistics = jnp.concatenate(stats, axis=1)
    kept, sent = together(*last_messages(jnp.concatenate(parts, axis=1), statistics))
    straight, crossed = together(across(kept, bits[-1], 0), across(sent, bits[-1], 1))
    return statistics, straight + crossed


def reduce_mixed(crossing, staying, cross_stats, stay_stats, bits):
    parts, stats = halve((crossing, staying), (cross_stats, stay_stats), bits)
    kept, sent = last_messages(parts[0], stats[0])
    stay_kept, stay_sent = last_messages(parts[1], stats[1])
    kept, sent, stay_sent = together(kept, sent, stay_sent)
    got = (
        across(kept, bits[-1], 0),
        across(sent, bits[-1], 1),
        swap(stay_sent, bits[-1]),
    )
    straight, crossed, got = together(*got)
    second = lax.axis_index("side") == 1
    return straight + crossed + jnp.where(second, stay_kept + got, 0.0)


def gather_moment(own, facing, bits):
    rows = facing.shape[0] - PAD
    chunk, facing = facing[:rows], facing[rows:]
    if own is None:
        chunk, facing = together(chunk, facing)
        got, own = together(swap(chunk, bits[-1]), swap(facing, "side"))
    else:
        got = swap(jnp.concatenate([chunk, own], axis=0), bits[-1])
        got, own = got[:rows], own + got[rows:]
    both = jnp.concatenate([own, facing], axis=0)
    value = jnp.concatenate([chunk, got], axis=0)
    half = value.shape[1] // 2
    parts = [value[:, :half], value[:, half:]]
    for stage in reversed(range(len(bits) - 1)):
        axes = stage_axes(bits, stage)
        if stage == 0:
            *parts, both = together(*parts, both)
            got = [swap(parts[i], axes[i]) for i in range(2)]
            *got, peer = together(*got, swap(both, "core"))
        else:
            parts = together(*parts)
            got = together(*(swap(parts[i], axes[i]) for i in range(2)))
        joined = []
        for i in range(2):
            if i == 1 and stage == 0:
                joined.append(join_inner(parts[i], got[i]))
            else:
                joined.append(jnp.concatenate([parts[i], got[i]], axis=0))
        parts = joined
    both = both + peer
    return jnp.concatenate(parts, axis=1), both[:PAD], both[PAD:]


def weigh(logits, mass, squares):
    scaled = jax.nn.softmax(logits, axis=1) * mass
    columns = jnp.sum(scaled, axis=0, keepdims=True)
    rank = scaled.shape[1]
    return scaled, jnp.concatenate(
        [
            jnp.sum(scaled * squares, axis=0, keepdims=True),
            columns,
            jnp.broadcast_to(jnp.sum(columns, axis=1, keepdims=True), columns.shape),
            jnp.zeros((PAD - 3, rank), jnp.float32),
        ],
        axis=0,
    )


def make_body(axes):
    bits = axes[2:][::-1]

    def body(points, log_factor, masses):
        return steps(points, log_factor, masses)

    def steps(points, log_factor, masses):
        source = lax.axis_index("side") == 0
        group = 2 * lax.axis_index("side") + lax.axis_index("core")
        rows, _ = points.shape
        rank = log_factor.shape[1]
        half = rows // 2
        devices = 1
        for axis in axes:
            devices *= lax.axis_size(axis)

        moved = move(points)
        squares = jnp.sum(points * points, axis=1, keepdims=True)
        mass = masses[:, None]
        near, far = arrange_base(points, bits)
        lanes = lax.broadcasted_iota(jnp.int32, (rows, 128), 1)
        packed = jnp.concatenate(
            [log_factor, jnp.where(lanes < 64, mass, squares)], axis=1
        )

        second_core = lax.axis_index("core") == 1
        scaled, statistics = weigh(log_factor, mass, squares)
        stay_stats = jnp.where(group == 2, statistics, 0.0)
        statistics = jnp.where(group == 2, 0.0, statistics)
        other = swap(contract_rows(far[:rows], scaled), "core")
        held, other = together(contract_rows(near[:rows], scaled), other)
        crossing = jnp.where(
            source, held + other, jnp.where(second_core, held, other)
        )
        staying = jnp.where(second_core, other, held)
        facing = reduce_mixed(crossing, staying, statistics, stay_stats, bits)
        moment, own, facing = gather_moment(None, facing, bits)

        first, second = move(packed)
        extra = jnp.where(group == 1, second, jnp.where(group == 3, packed[half:], first))
        near, far = arrange_extra(points, *moved, near, far, bits)
        logits = jnp.concatenate([log_factor, extra[:, :rank]], axis=0)
        mass = jnp.concatenate(
            [jnp.where(source, mass, 0.0), extra[:, rank : rank + 1]], axis=0
        )
        squares = jnp.concatenate([squares, extra[:, rank + 64 : rank + 65]], axis=0)
        real = source | (lax.broadcasted_iota(jnp.int32, (logits.shape[0], 1), 0) >= rows)

        for iteration in range(ITERS):
            if iteration:
                scaled, statistics = weigh(logits, mass, squares)
                other = swap(contract_rows(far, scaled), "core")
                held, other = together(contract_rows(near, scaled), other)
                own, facing = reduce_moment(held + other, statistics, bits)
                moment, own, facing = gather_moment(own, facing, bits)
            cross, other = together(times(near, moment), swap(moment, "core"))
            cross = cross + times(far, other)
            share = facing[1:2] / facing[2:3]
            marginal = 0.5 * (own[1:2] / own[2:3] + share)
            gradient = (
                squares * share - 2.0 * (cross / facing[2:3]) + facing[0:1] / facing[2:3]
            ) / marginal
            centred = gradient - jnp.mean(gradient, axis=1, keepdims=True)
            largest = jnp.max(jnp.where(real, jnp.abs(centred), 0.0))
            spread = jnp.full((devices, 128), largest, jnp.float32)
            largest = jnp.max(lax.all_to_all(spread, axes, 0, 0, tiled=True))
            logits = logits - step_scale / (largest + 1e-06) * gradient
        factors = rank * jax.nn.softmax(logits, axis=1)
        return from_side(factors[:rows], factors[rows:])

    return body


def solution(mesh):
    pts = mesh.shape["pts"]
    count = pts.bit_length() - 1
    axes = ("side", "core") + tuple(f"bit{i}" for i in reversed(range(count)))
    split = Mesh(mesh.devices.reshape((2,) * len(axes)), axes)
    in_specs = (P(axes, None), P(axes, None), P(axes))
    return jax.shard_map(
        make_body(axes), mesh=split, in_specs=in_specs, out_specs=P(axes, None), check_vma=False
    )
```

```python
import functools

import jax
import jax.numpy as jnp
from jax import lax
from jax.experimental import pallas as pl
from jax.experimental.pallas import tpu as pltpu
from jax.sharding import Mesh, PartitionSpec as P


ITERS = 2

step_scale = 4.0
highest = lax.Precision.HIGHEST
PAD = 8


def swap(value, axis):
    return lax.ppermute(value, axis, [(0, 1), (1, 0)])


def together(*values):
    return lax.optimization_barrier(values)


def contract_rows(left, right):
    return lax.dot_general(
        left,
        right,
        (((0,), (0,)), ((), ())),
        precision=highest,
        preferred_element_type=jnp.float32,
    )


def times(left, right):
    return jnp.dot(left, right, precision=highest, preferred_element_type=jnp.float32)


def own_place(bits):
    place = lax.axis_index("core")
    for axis in bits:
        place = 2 * place + lax.axis_index(axis)
    return place


def column_copies(source, begin, parts, place, sems):
    count = sems.shape[0]
    width = source.shape[1] // count
    rows = parts[0].shape[0]
    copies = []
    for i in range(count):
        column = pl.multiple_of((i ^ place) * width, width)
        copies.append(
            pltpu.make_async_copy(
                source.at[pl.ds(begin, rows), pl.ds(column, width)],
                parts[2 * i // count].at[:, pl.ds(i % (count // 2) * width, width)],
                sems.at[i],
            )
        )
    return copies


def row_copies(parts, targets, top, sems):
    rows = parts[0].shape[0]
    return [
        pltpu.make_async_copy(parts[i], targets[i].at[pl.ds(top, rows), :], sems.at[i])
        for i in range(2)
    ]


def base_kernel(bits, points, near, far, squares, near_part, far_part, sems, out_sems):
    parts = near_part, far_part
    copies = column_copies(points, 0, parts, own_place(bits), sems)
    for copy in copies:
        copy.start()
    for copy in copies:
        copy.wait()
    copies = row_copies(parts, (near, far), 0, out_sems)
    for copy in copies:
        copy.start()
    total = jnp.zeros_like(squares)
    for part in parts:
        for begin in range(0, part.shape[1], 128):
            block = part[:, begin : begin + 128]
            total = total + block * block
    squares[...] = total
    for copy in copies:
        copy.wait()


def extra_kernel(
    bits, points, first, second, near_in, far_in, near, far, near_part, far_part, sems, out_sems
):
    del near_in, far_in
    parts = near_part, far_part
    place = own_place(bits)
    group = 2 * lax.axis_index("side") + lax.axis_index("core")
    half = first.shape[0]

    @pl.when((group == 0) | (group == 2))
    def _():
        for copy in column_copies(first, 0, parts, place, sems):
            copy.start()

    @pl.when(group == 1)
    def _():
        for copy in column_copies(second, 0, parts, place, sems):
            copy.start()

    @pl.when(group == 3)
    def _():
        for copy in column_copies(points, half, parts, place, sems):
            copy.start()

    for copy in column_copies(first, 0, parts, place, sems):
        copy.wait()
    copies = row_copies(parts, (near, far), points.shape[0], out_sems)
    for copy in copies:
        copy.start()
    for copy in copies:
        copy.wait()


def arrange_base(points, bits):
    rows, width = points.shape
    blocks = 2 ** (1 + len(bits))
    if (width // blocks) % 128:
        near, far = reorder(points, bits)
        return near, far, jnp.sum(points * points, axis=1, keepdims=True)
    near, far, sums = arrange_call(base_kernel, points, rows, bits, {})(points)
    return near, far, jnp.sum(sums, axis=1, keepdims=True)


def reorder(points, bits):
    rows, width = points.shape
    blocks = 2 ** (1 + len(bits))
    order = jnp.arange(blocks) ^ own_place(bits)
    whole = points.reshape(rows, blocks, -1)[:, order].reshape(rows, width)
    return whole[:, : width // 2], whole[:, width // 2 :]


def arrange_extra(points, first, second, near, far, bits):
    rows, width = points.shape
    blocks = 2 ** (1 + len(bits))
    half = rows // 2
    if (width // blocks) % 128:
        group = 2 * lax.axis_index("side") + lax.axis_index("core")
        extra = jnp.where(group == 1, second, jnp.where(group == 3, points[half:], first))
        extra = reorder(extra, bits)
        return tuple(jnp.concatenate(pair, axis=0) for pair in zip((near, far), extra))
    return arrange_call(extra_kernel, points, half, bits, {3: 0, 4: 1})(
        points, first, second, near, far
    )


def arrange_call(kernel, points, count, bits, aliases):
    rows, width = points.shape
    anywhere = pl.BlockSpec(memory_space=pl.ANY)
    shape = jax.ShapeDtypeStruct((rows + rows // 2, width // 2), points.dtype)
    part = pltpu.VMEM((count, width // 2), points.dtype)
    shapes, specs = (shape, shape), (anywhere, anywhere)
    if not aliases:
        shapes += (jax.ShapeDtypeStruct((count, 128), points.dtype),)
        specs += (pl.BlockSpec(memory_space=pltpu.VMEM),)
    return pl.pallas_call(
        functools.partial(kernel, bits),
        out_shape=shapes,
        in_specs=[anywhere] * (5 if aliases else 1),
        out_specs=specs,
        scratch_shapes=[
            part,
            part,
            pltpu.SemaphoreType.DMA((2 ** (1 + len(bits)),)),
            pltpu.SemaphoreType.DMA((2,)),
        ],
        input_output_aliases=aliases,
    )


def move(own):
    half = own.shape[0] // 2
    own, head = together(own, own[:half])
    first = lax.ppermute(head, ("side", "core"), [(2, 0), (3, 2)])
    second = lax.ppermute(own[half:], ("side", "core"), [(2, 1)])
    return first, second


def from_side(base, extra):
    group = 2 * lax.axis_index("side") + lax.axis_index("core")
    half = extra.shape[0]
    first = lax.ppermute(extra, ("side", "core"), [(0, 2), (2, 3)])
    second = lax.ppermute(extra, ("side", "core"), [(1, 2)])
    top = jnp.where(group < 2, base[:half], first)
    bottom = jnp.where(group < 2, base[half:], jnp.where(group == 2, second, extra))
    return jnp.concatenate([top, bottom], axis=0)


def outer_halves(value):
    half = value.shape[0] // 2
    return value[:half], value[half:]


def inner_halves(value):
    rows, columns = value.shape
    value = value.reshape(2, 2, rows // 4, columns)
    return value[:, 0].reshape(-1, columns), value[:, 1].reshape(-1, columns)


def join_inner(mine, got):
    rows, columns = mine.shape
    blocks = [v.reshape(2, 1, rows // 2, columns) for v in (mine, got)]
    return jnp.concatenate(blocks, axis=1).reshape(2 * rows, columns)


def across(value, axis, flip):
    pairs = [(i, (i ^ 2) ^ flip) for i in range(4)]
    return lax.ppermute(value, ("side", axis), pairs)


def stage_axes(bits, stage):
    if stage < 2:
        return bits[stage], bits[1 - stage]
    return bits[stage], bits[stage]


def halve(parts, stats, bits):
    parts, stats = list(parts), list(stats)
    for stage in range(len(bits) - 1):
        axes = stage_axes(bits, stage)
        kept, sent = [None, None], [None, None]
        for i in range(2):
            inner = i == 1 and stage == 0
            kept[i], sent[i] = (inner_halves if inner else outer_halves)(parts[i])
            sent[i] = jnp.concatenate([sent[i], stats[i]], axis=0)
        sent = together(*sent)
        got = [swap(sent[i], axes[i]) for i in range(2)]
        got = together(*got)
        for i in range(2):
            rows = kept[i].shape[0]
            parts[i] = kept[i] + got[i][:rows]
            stats[i] = stats[i] + got[i][rows:]
    return parts, stats


def last_messages(part, stats):
    kept, sent = outer_halves(part)
    return jnp.concatenate([kept, stats], axis=0), jnp.concatenate([sent, stats], axis=0)


def reduce_moment(held, statistics, bits):
    half = held.shape[1] // 2
    parts, stats = halve(
        (held[:, :half], held[:, half:]),
        (statistics[:, :half], statistics[:, half:]),
        bits,
    )
    statistics = jnp.concatenate(stats, axis=1)
    kept, sent = together(*last_messages(jnp.concatenate(parts, axis=1), statistics))
    straight, crossed = together(across(kept, bits[-1], 0), across(sent, bits[-1], 1))
    return statistics, straight + crossed


def reduce_mixed(crossing, staying, cross_stats, stay_stats, bits):
    parts, stats = halve((crossing, staying), (cross_stats, stay_stats), bits)
    kept, sent = last_messages(parts[0], stats[0])
    stay_kept, stay_sent = last_messages(parts[1], stats[1])
    kept, sent, stay_sent = together(kept, sent, stay_sent)
    got = (
        across(kept, bits[-1], 0),
        across(sent, bits[-1], 1),
        swap(stay_sent, bits[-1]),
    )
    straight, crossed, got = together(*got)
    second = lax.axis_index("side") == 1
    return straight + crossed + jnp.where(second, stay_kept + got, 0.0)


def gather_moment(own, facing, bits):
    rows = facing.shape[0] - PAD
    chunk, facing = facing[:rows], facing[rows:]
    if own is None:
        chunk, facing = together(chunk, facing)
        got, own = together(swap(chunk, bits[-1]), swap(facing, "side"))
    else:
        got = swap(jnp.concatenate([chunk, own], axis=0), bits[-1])
        got, own = got[:rows], own + got[rows:]
    both = jnp.concatenate([own, facing], axis=0)
    value = jnp.concatenate([chunk, got], axis=0)
    half = value.shape[1] // 2
    parts = [value[:, :half], value[:, half:]]
    for stage in reversed(range(len(bits) - 1)):
        axes = stage_axes(bits, stage)
        if stage == 0:
            *parts, both = together(*parts, both)
            got = [swap(parts[i], axes[i]) for i in range(2)]
            *got, peer = together(*got, swap(both, "core"))
        else:
            parts = together(*parts)
            got = together(*(swap(parts[i], axes[i]) for i in range(2)))
        joined = []
        for i in range(2):
            if i == 1 and stage == 0:
                joined.append(join_inner(parts[i], got[i]))
            else:
                joined.append(jnp.concatenate([parts[i], got[i]], axis=0))
        parts = joined
    both = both + peer
    return jnp.concatenate(parts, axis=1), both[:PAD], both[PAD:]


def weigh(logits, mass, squares, totals):
    scaled = jax.nn.softmax(logits, axis=1) * mass
    columns = jnp.sum(scaled, axis=0, keepdims=True)
    sums = [jnp.sum(scaled * squares, axis=0, keepdims=True), columns]
    if totals:
        total = jnp.sum(columns, axis=1, keepdims=True)
        sums.append(jnp.broadcast_to(total, columns.shape))
    rest = PAD - len(sums)
    return scaled, jnp.concatenate([*sums, jnp.zeros((rest, columns.shape[1]))], axis=0)


def make_body(axes):
    bits = axes[2:][::-1]

    def body(points, log_factor, masses):
        return steps(points, log_factor, masses)

    def steps(points, log_factor, masses):
        source = lax.axis_index("side") == 0
        group = 2 * lax.axis_index("side") + lax.axis_index("core")
        rows, _ = points.shape
        rank = log_factor.shape[1]
        half = rows // 2
        devices = 1
        for axis in axes:
            devices *= lax.axis_size(axis)

        moved = move(points)
        mass = masses[:, None]
        near, far, squares = arrange_base(points, bits)
        lanes = lax.broadcasted_iota(jnp.int32, (rows, 128), 1)
        packed = jnp.concatenate(
            [log_factor, jnp.where(lanes < 64, mass, squares)], axis=1
        )

        second_core = lax.axis_index("core") == 1
        scaled, statistics = weigh(log_factor, mass, squares, True)
        stay_stats = jnp.where(group == 2, statistics, 0.0)
        statistics = jnp.where(group == 2, 0.0, statistics)
        other = swap(contract_rows(far[:rows], scaled), "core")
        held, other = together(contract_rows(near[:rows], scaled), other)
        crossing = jnp.where(
            source, held + other, jnp.where(second_core, held, other)
        )
        staying = jnp.where(second_core, other, held)
        facing = reduce_mixed(crossing, staying, statistics, stay_stats, bits)
        moment, own, facing = gather_moment(None, facing, bits)

        first, second = move(packed)
        extra = jnp.where(group == 1, second, jnp.where(group == 3, packed[half:], first))
        near, far = arrange_extra(points, *moved, near, far, bits)
        logits = jnp.concatenate([log_factor, extra[:, :rank]], axis=0)
        mass = jnp.concatenate(
            [jnp.where(source, mass, 0.0), extra[:, rank : rank + 1]], axis=0
        )
        squares = jnp.concatenate([squares, extra[:, rank + 64 : rank + 65]], axis=0)
        real = source | (lax.broadcasted_iota(jnp.int32, (logits.shape[0], 1), 0) >= rows)

        own_mass, mass_total = own[2:3], facing[2:3]
        for iteration in range(ITERS):
            if iteration:
                scaled, statistics = weigh(logits, mass, squares, False)
                other = swap(contract_rows(far, scaled), "core")
                held, other = together(contract_rows(near, scaled), other)
                own, facing = reduce_moment(held + other, statistics, bits)
                moment, own, facing = gather_moment(own, facing, bits)
            cross, other = together(times(near, moment), swap(moment, "core"))
            cross = cross + times(far, other)
            share = facing[1:2] / mass_total
            marginal = 0.5 * (own[1:2] / own_mass + share)
            gradient = (
                squares * share - 2.0 * (cross / mass_total) + facing[0:1] / mass_total
            ) / marginal
            centred = gradient - jnp.mean(gradient, axis=1, keepdims=True)
            largest = jnp.max(jnp.where(real, jnp.abs(centred), 0.0))
            spread = jnp.full((devices, 128), largest, jnp.float32)
            largest = jnp.max(lax.all_to_all(spread, axes, 0, 0, tiled=True), axis=0)
            rate = jnp.tile(step_scale / (largest + 1e-06), rank // 128)
            logits = logits - rate[None, :] * gradient
        factors = rank * jax.nn.softmax(logits, axis=1)
        return from_side(factors[:rows], factors[rows:])

    return body


def solution(mesh):
    pts = mesh.shape["pts"]
    count = pts.bit_length() - 1
    axes = ("side", "core") + tuple(f"bit{i}" for i in reversed(range(count)))
    split = Mesh(mesh.devices.reshape((2,) * len(axes)), axes)
    in_specs = (P(axes, None), P(axes, None), P(axes))
    return jax.shard_map(
        make_body(axes), mesh=split, in_specs=in_specs, out_specs=P(axes, None), check_vma=False
    )
```

```python
import functools

import jax
import jax.numpy as jnp
from jax import lax
from jax.experimental import pallas as pl
from jax.experimental.pallas import tpu as pltpu
from jax.sharding import Mesh, PartitionSpec as P


ITERS = 2

step_scale = 4.0
highest = lax.Precision.HIGHEST
PAD = 8


def swap(value, axis):
    return lax.ppermute(value, axis, [(0, 1), (1, 0)])


def together(*values):
    return lax.optimization_barrier(values)


def in_lanes(column, lanes):
    return lax.optimization_barrier(jnp.broadcast_to(column, (column.shape[0], lanes)))


def contract_rows(left, right):
    return lax.dot_general(
        left,
        right,
        (((0,), (0,)), ((), ())),
        precision=highest,
        preferred_element_type=jnp.float32,
    )


def times(left, right):
    return jnp.dot(left, right, precision=highest, preferred_element_type=jnp.float32)


def own_place(bits):
    place = lax.axis_index("core")
    for axis in bits:
        place = 2 * place + lax.axis_index(axis)
    return place


def column_copies(source, begin, parts, place, sems):
    count = sems.shape[0]
    width = source.shape[1] // count
    rows = parts[0].shape[0]
    copies = []
    for i in range(count):
        column = pl.multiple_of((i ^ place) * width, width)
        copies.append(
            pltpu.make_async_copy(
                source.at[pl.ds(begin, rows), pl.ds(column, width)],
                parts[2 * i // count].at[:, pl.ds(i % (count // 2) * width, width)],
                sems.at[i],
            )
        )
    return copies


def row_copies(parts, targets, top, sems):
    rows = parts[0].shape[0]
    return [
        pltpu.make_async_copy(parts[i], targets[i].at[pl.ds(top, rows), :], sems.at[i])
        for i in range(2)
    ]


def base_kernel(bits, points, near, far, near_part, far_part, squares, sems, out_sems):
    parts = near_part, far_part
    copies = column_copies(points, 0, parts, own_place(bits), sems)
    for copy in copies:
        copy.start()
    for copy in copies:
        copy.wait()
    copies = row_copies(parts, (near, far), 0, out_sems)
    for copy in copies:
        copy.start()
    total = jnp.zeros_like(squares)
    for part in parts:
        for begin in range(0, part.shape[1], 128):
            block = part[:, begin : begin + 128]
            total = total + block * block
    squares[...] = total
    for copy in copies:
        copy.wait()


def extra_kernel(
    bits, points, first, second, near_in, far_in, near, far, near_part, far_part, sems, out_sems
):
    del near_in, far_in
    parts = near_part, far_part
    place = own_place(bits)
    group = 2 * lax.axis_index("side") + lax.axis_index("core")
    half = first.shape[0]

    @pl.when((group == 0) | (group == 2))
    def _():
        for copy in column_copies(first, 0, parts, place, sems):
            copy.start()

    @pl.when(group == 1)
    def _():
        for copy in column_copies(second, 0, parts, place, sems):
            copy.start()

    @pl.when(group == 3)
    def _():
        for copy in column_copies(points, half, parts, place, sems):
            copy.start()

    for copy in column_copies(first, 0, parts, place, sems):
        copy.wait()
    copies = row_copies(parts, (near, far), points.shape[0], out_sems)
    for copy in copies:
        copy.start()
    for copy in copies:
        copy.wait()


def arrange_base(points, bits):
    rows, width = points.shape
    blocks = 2 ** (1 + len(bits))
    if (width // blocks) % 128:
        near, far = reorder(points, bits)
        return near, far, near, far, jnp.sum(points * points, axis=1, keepdims=True)
    anywhere = pl.BlockSpec(memory_space=pl.ANY)
    inside = pl.BlockSpec(memory_space=pltpu.VMEM)
    whole = pltpu.HBM((rows + rows // 2, width // 2), points.dtype)
    part = pltpu.VMEM((rows, width // 2), points.dtype)
    *arrays, sums = pl.pallas_call(
        functools.partial(base_kernel, bits),
        out_shape=(whole, whole, part, part, pltpu.VMEM((rows, 128), points.dtype)),
        in_specs=[anywhere],
        out_specs=(anywhere, anywhere, inside, inside, inside),
        scratch_shapes=[pltpu.SemaphoreType.DMA((blocks,)), pltpu.SemaphoreType.DMA((2,))],
        compiler_params=pltpu.CompilerParams(vmem_limit_bytes=4 << 20),
        name="base_rows",
    )(pltpu.with_memory_space_constraint(points, pltpu.HBM))
    return *arrays, jnp.sum(sums, axis=1, keepdims=True)


def reorder(points, bits):
    rows, width = points.shape
    blocks = 2 ** (1 + len(bits))
    order = jnp.arange(blocks) ^ own_place(bits)
    whole = points.reshape(rows, blocks, -1)[:, order].reshape(rows, width)
    return whole[:, : width // 2], whole[:, width // 2 :]


def arrange_extra(points, first, second, near, far, bits):
    rows, width = points.shape
    blocks = 2 ** (1 + len(bits))
    half = rows // 2
    if (width // blocks) % 128:
        group = 2 * lax.axis_index("side") + lax.axis_index("core")
        extra = jnp.where(group == 1, second, jnp.where(group == 3, points[half:], first))
        extra = reorder(extra, bits)
        return tuple(jnp.concatenate(pair, axis=0) for pair in zip((near, far), extra))
    return arrange_call(extra_kernel, points, half, bits, {3: 0, 4: 1})(
        pltpu.with_memory_space_constraint(points, pltpu.HBM), first, second, near, far
    )


def arrange_call(kernel, points, count, bits, aliases):
    rows, width = points.shape
    anywhere = pl.BlockSpec(memory_space=pl.ANY)
    shape = jax.ShapeDtypeStruct((rows + rows // 2, width // 2), points.dtype)
    part = pltpu.VMEM((count, width // 2), points.dtype)
    return pl.pallas_call(
        functools.partial(kernel, bits),
        out_shape=(shape, shape),
        in_specs=[anywhere] * 5,
        out_specs=(anywhere, anywhere),
        scratch_shapes=[
            part,
            part,
            pltpu.SemaphoreType.DMA((2 ** (1 + len(bits)),)),
            pltpu.SemaphoreType.DMA((2,)),
        ],
        input_output_aliases=aliases,
    )


def move(own):
    half = own.shape[0] // 2
    own, head = together(own, own[:half])
    first = lax.ppermute(head, ("side", "core"), [(2, 0), (3, 2)])
    second = lax.ppermute(own[half:], ("side", "core"), [(2, 1)])
    return first, second


def from_side(base, extra):
    group = 2 * lax.axis_index("side") + lax.axis_index("core")
    half = extra.shape[0]
    first = lax.ppermute(extra, ("side", "core"), [(0, 2), (2, 3)])
    second = lax.ppermute(extra, ("side", "core"), [(1, 2)])
    top = jnp.where(group < 2, base[:half], first)
    bottom = jnp.where(group < 2, base[half:], jnp.where(group == 2, second, extra))
    return jnp.concatenate([top, bottom], axis=0)


def outer_halves(value):
    half = value.shape[0] // 2
    return value[:half], value[half:]


def inner_halves(value):
    rows, columns = value.shape
    value = value.reshape(2, 2, rows // 4, columns)
    return value[:, 0].reshape(-1, columns), value[:, 1].reshape(-1, columns)


def join_inner(mine, got):
    rows, columns = mine.shape
    blocks = [v.reshape(2, 1, rows // 2, columns) for v in (mine, got)]
    return jnp.concatenate(blocks, axis=1).reshape(2 * rows, columns)


def across(value, axis, flip):
    pairs = [(i, (i ^ 2) ^ flip) for i in range(4)]
    return lax.ppermute(value, ("side", axis), pairs)


def stage_axes(bits, stage):
    if stage < 2:
        return bits[stage], bits[1 - stage]
    return bits[stage], bits[stage]


def halve(parts, stats, bits):
    parts, stats = list(parts), list(stats)
    for stage in range(len(bits) - 1):
        axes = stage_axes(bits, stage)
        kept, sent = [None, None], [None, None]
        for i in range(2):
            inner = i == 1 and stage == 0
            kept[i], sent[i] = (inner_halves if inner else outer_halves)(parts[i])
            sent[i] = jnp.concatenate([sent[i], stats[i]], axis=0)
        sent = together(*sent)
        got = [swap(sent[i], axes[i]) for i in range(2)]
        got = together(*got)
        for i in range(2):
            rows = kept[i].shape[0]
            parts[i] = kept[i] + got[i][:rows]
            stats[i] = stats[i] + got[i][rows:]
    return parts, stats


def last_messages(part, stats):
    kept, sent = outer_halves(part)
    return jnp.concatenate([kept, stats], axis=0), jnp.concatenate([sent, stats], axis=0)


def reduce_moment(held, statistics, bits):
    half = held.shape[1] // 2
    parts, stats = halve(
        (held[:, :half], held[:, half:]),
        (statistics[:, :half], statistics[:, half:]),
        bits,
    )
    statistics = jnp.concatenate(stats, axis=1)
    kept, sent = together(*last_messages(jnp.concatenate(parts, axis=1), statistics))
    straight, crossed = together(across(kept, bits[-1], 0), across(sent, bits[-1], 1))
    return statistics, straight + crossed


def reduce_mixed(crossing, staying, cross_stats, stay_stats, bits):
    parts, stats = halve((crossing, staying), (cross_stats, stay_stats), bits)
    kept, sent = last_messages(parts[0], stats[0])
    stay_kept, stay_sent = last_messages(parts[1], stats[1])
    kept, sent, stay_sent = together(kept, sent, stay_sent)
    got = (
        across(kept, bits[-1], 0),
        across(sent, bits[-1], 1),
        swap(stay_sent, bits[-1]),
    )
    straight, crossed, got = together(*got)
    second = lax.axis_index("side") == 1
    return straight + crossed + jnp.where(second, stay_kept + got, 0.0)


def gather_moment(own, facing, bits):
    rows = facing.shape[0] - PAD
    chunk, facing = facing[:rows], facing[rows:]
    if own is None:
        chunk, facing = together(chunk, facing)
        got, own = together(swap(chunk, bits[-1]), swap(facing, "side"))
    else:
        got = swap(jnp.concatenate([chunk, own], axis=0), bits[-1])
        got, own = got[:rows], own + got[rows:]
    both = jnp.concatenate([own, facing], axis=0)
    value = jnp.concatenate([chunk, got], axis=0)
    half = value.shape[1] // 2
    parts = [value[:, :half], value[:, half:]]
    for stage in reversed(range(len(bits) - 1)):
        axes = stage_axes(bits, stage)
        if stage == 0:
            *parts, both = together(*parts, both)
            got = [swap(parts[i], axes[i]) for i in range(2)]
            *got, peer = together(*got, swap(both, "core"))
        else:
            parts = together(*parts)
            got = together(*(swap(parts[i], axes[i]) for i in range(2)))
        joined = []
        for i in range(2):
            if i == 1 and stage == 0:
                joined.append(join_inner(parts[i], got[i]))
            else:
                joined.append(jnp.concatenate([parts[i], got[i]], axis=0))
        parts = joined
    both = both + peer
    return jnp.concatenate(parts, axis=1), both[:PAD], both[PAD:]


def weigh(logits, mass, squares, totals):
    scaled = jax.nn.softmax(logits, axis=1) * mass
    columns = jnp.sum(scaled, axis=0, keepdims=True)
    sums = [jnp.sum(scaled * squares, axis=0, keepdims=True), columns]
    if totals:
        total = in_lanes(jnp.sum(scaled, axis=1, keepdims=True), columns.shape[1])
        sums.append(jnp.sum(total, axis=0, keepdims=True))
    rest = PAD - len(sums)
    return scaled, jnp.concatenate([*sums, jnp.zeros((rest, columns.shape[1]))], axis=0)


def make_body(axes):
    bits = axes[2:][::-1]

    def body(points, log_factor, masses):
        return steps(points, log_factor, masses)

    def steps(points, log_factor, masses):
        source = lax.axis_index("side") == 0
        group = 2 * lax.axis_index("side") + lax.axis_index("core")
        rows, _ = points.shape
        rank = log_factor.shape[1]
        half = rows // 2
        devices = 1
        for axis in axes:
            devices *= lax.axis_size(axis)

        moved = move(points)
        mass = masses[:, None]
        near, far, near_base, far_base, squares = arrange_base(points, bits)
        lanes = lax.broadcasted_iota(jnp.int32, (rows, 128), 1)
        packed = jnp.concatenate(
            [log_factor, jnp.where(lanes < 64, mass, squares)], axis=1
        )

        second_core = lax.axis_index("core") == 1
        scaled, statistics = weigh(log_factor, mass, squares, True)
        stay_stats = jnp.where(group == 2, statistics, 0.0)
        statistics = jnp.where(group == 2, 0.0, statistics)
        other = swap(contract_rows(far_base, scaled), "core")
        held, other = together(contract_rows(near_base, scaled), other)
        crossing = jnp.where(
            source, held + other, jnp.where(second_core, held, other)
        )
        staying = jnp.where(second_core, other, held)
        facing = reduce_mixed(crossing, staying, statistics, stay_stats, bits)
        moment, own, facing = gather_moment(None, facing, bits)

        first, second = move(packed)
        extra = jnp.where(group == 1, second, jnp.where(group == 3, packed[half:], first))
        near, far = arrange_extra(points, *moved, near, far, bits)
        logits = jnp.concatenate([log_factor, extra[:, :rank]], axis=0)
        mass = jnp.concatenate(
            [jnp.where(source, mass, 0.0), extra[:, rank : rank + 1]], axis=0
        )
        squares = jnp.concatenate([squares, extra[:, rank + 64 : rank + 65]], axis=0)
        real = source | (lax.broadcasted_iota(jnp.int32, (logits.shape[0], 1), 0) >= rows)

        own_mass, mass_total = own[2:3], facing[2:3]
        for iteration in range(ITERS):
            if iteration:
                scaled, statistics = weigh(logits, mass, squares, False)
                other = swap(contract_rows(far, scaled), "core")
                held, other = together(contract_rows(near, scaled), other)
                own, facing = reduce_moment(held + other, statistics, bits)
                moment, own, facing = gather_moment(own, facing, bits)
            cross, other = together(times(near, moment), swap(moment, "core"))
            cross = cross + times(far, other)
            share = facing[1:2] / mass_total
            marginal = 0.5 * (own[1:2] / own_mass + share)
            gradient = (
                squares * share - 2.0 * (cross / mass_total) + facing[0:1] / mass_total
            ) / marginal
            centred = gradient - jnp.mean(gradient, axis=1, keepdims=True)
            largest = jnp.max(jnp.where(real, jnp.abs(centred), 0.0), axis=1, keepdims=True)
            largest = jnp.max(in_lanes(largest, 128), axis=0, keepdims=True)
            spread = jnp.broadcast_to(largest, (devices, 128))
            largest = jnp.max(lax.all_to_all(spread, axes, 0, 0, tiled=True), axis=0)
            rate = jnp.tile(step_scale / (largest + 1e-06), rank // 128)
            logits = logits - rate[None, :] * gradient
        factors = rank * jax.nn.softmax(logits, axis=1)
        return from_side(factors[:rows], factors[rows:])

    return body


def solution(mesh):
    pts = mesh.shape["pts"]
    count = pts.bit_length() - 1
    axes = ("side", "core") + tuple(f"bit{i}" for i in reversed(range(count)))
    split = Mesh(mesh.devices.reshape((2,) * len(axes)), axes)
    in_specs = (P(axes, None), P(axes, None), P(axes))
    return jax.shard_map(
        make_body(axes), mesh=split, in_specs=in_specs, out_specs=P(axes, None), check_vma=False
    )
```

```python
import functools

import jax
import jax.numpy as jnp
from jax import lax
from jax.experimental import pallas as pl
from jax.experimental.pallas import tpu as pltpu
from jax.sharding import Mesh, PartitionSpec as P


ITERS = 2

step_scale = 4.0
highest = lax.Precision.HIGHEST
PAD = 8


def swap(value, axis):
    return lax.ppermute(value, axis, [(0, 1), (1, 0)])


def together(*values):
    return lax.optimization_barrier(values)


def in_lanes(column, lanes):
    return lax.optimization_barrier(jnp.broadcast_to(column, (column.shape[0], lanes)))


def contract_rows(left, right):
    return lax.dot_general(
        left,
        right,
        (((0,), (0,)), ((), ())),
        precision=highest,
        preferred_element_type=jnp.float32,
    )


def times(left, right):
    return jnp.dot(left, right, precision=highest, preferred_element_type=jnp.float32)


def own_place(bits):
    place = lax.axis_index("core")
    for axis in bits:
        place = 2 * place + lax.axis_index(axis)
    return place


def column_copies(source, begin, parts, place, sems):
    count = sems.shape[0]
    width = source.shape[1] // count
    rows = parts[0].shape[0]
    copies = []
    for i in range(count):
        column = pl.multiple_of((i ^ place) * width, width)
        copies.append(
            pltpu.make_async_copy(
                source.at[pl.ds(begin, rows), pl.ds(column, width)],
                parts[2 * i // count].at[:, pl.ds(i % (count // 2) * width, width)],
                sems.at[i],
            )
        )
    return copies


def row_copies(parts, targets, top, sems):
    rows = parts[0].shape[0]
    return [
        pltpu.make_async_copy(parts[i], targets[i].at[pl.ds(top, rows), :], sems.at[i])
        for i in range(2)
    ]


def base_kernel(bits, points, near, far, far_part, squares, near_part, sems, out_sems):
    parts = near_part, far_part
    copies = column_copies(points, 0, parts, own_place(bits), sems)
    for copy in copies:
        copy.start()
    for copy in copies:
        copy.wait()
    copies = row_copies(parts, (near, far), 0, out_sems)
    for copy in copies:
        copy.start()
    total = jnp.zeros_like(squares)
    for part in parts:
        for begin in range(0, part.shape[1], 128):
            block = part[:, begin : begin + 128]
            total = total + block * block
    squares[...] = total
    for copy in copies:
        copy.wait()


def extra_kernel(
    bits, points, first, second, near_in, far_in, near, far, near_part, far_part, sems, out_sems
):
    del near_in, far_in
    parts = near_part, far_part
    place = own_place(bits)
    group = 2 * lax.axis_index("side") + lax.axis_index("core")
    half = first.shape[0]

    @pl.when((group == 0) | (group == 2))
    def _():
        for copy in column_copies(first, 0, parts, place, sems):
            copy.start()

    @pl.when(group == 1)
    def _():
        for copy in column_copies(second, 0, parts, place, sems):
            copy.start()

    @pl.when(group == 3)
    def _():
        for copy in column_copies(points, half, parts, place, sems):
            copy.start()

    for copy in column_copies(first, 0, parts, place, sems):
        copy.wait()
    copies = row_copies(parts, (near, far), points.shape[0], out_sems)
    for copy in copies:
        copy.start()
    for copy in copies:
        copy.wait()


def arrange_base(points, bits):
    rows, width = points.shape
    blocks = 2 ** (1 + len(bits))
    if (width // blocks) % 128:
        near, far = reorder(points, bits)
        return near, far, far, jnp.sum(points * points, axis=1, keepdims=True)
    anywhere = pl.BlockSpec(memory_space=pl.ANY)
    inside = pl.BlockSpec(memory_space=pltpu.VMEM)
    whole = pltpu.HBM((rows + rows // 2, width // 2), points.dtype)
    part = pltpu.VMEM((rows, width // 2), points.dtype)
    *arrays, sums = pl.pallas_call(
        functools.partial(base_kernel, bits),
        out_shape=(whole, whole, part, pltpu.VMEM((rows, 128), points.dtype)),
        in_specs=[anywhere],
        out_specs=(anywhere, anywhere, inside, inside),
        scratch_shapes=[
            part,
            pltpu.SemaphoreType.DMA((blocks,)),
            pltpu.SemaphoreType.DMA((2,)),
        ],
        compiler_params=pltpu.CompilerParams(vmem_limit_bytes=4 << 20),
        name="base_rows",
    )(pltpu.with_memory_space_constraint(points, pltpu.HBM))
    return *arrays, jnp.sum(sums, axis=1, keepdims=True)


def reorder(points, bits):
    rows, width = points.shape
    blocks = 2 ** (1 + len(bits))
    order = jnp.arange(blocks) ^ own_place(bits)
    whole = points.reshape(rows, blocks, -1)[:, order].reshape(rows, width)
    return whole[:, : width // 2], whole[:, width // 2 :]


def arrange_extra(points, first, second, near, far, bits):
    rows, width = points.shape
    blocks = 2 ** (1 + len(bits))
    half = rows // 2
    if (width // blocks) % 128:
        group = 2 * lax.axis_index("side") + lax.axis_index("core")
        extra = jnp.where(group == 1, second, jnp.where(group == 3, points[half:], first))
        extra = reorder(extra, bits)
        return tuple(jnp.concatenate(pair, axis=0) for pair in zip((near, far), extra))
    return arrange_call(extra_kernel, points, half, bits, {3: 0, 4: 1})(
        pltpu.with_memory_space_constraint(points, pltpu.HBM), first, second, near, far
    )


def arrange_call(kernel, points, count, bits, aliases):
    rows, width = points.shape
    anywhere = pl.BlockSpec(memory_space=pl.ANY)
    shape = jax.ShapeDtypeStruct((rows + rows // 2, width // 2), points.dtype)
    part = pltpu.VMEM((count, width // 2), points.dtype)
    return pl.pallas_call(
        functools.partial(kernel, bits),
        out_shape=(shape, shape),
        in_specs=[anywhere] * 5,
        out_specs=(anywhere, anywhere),
        scratch_shapes=[
            part,
            part,
            pltpu.SemaphoreType.DMA((2 ** (1 + len(bits)),)),
            pltpu.SemaphoreType.DMA((2,)),
        ],
        input_output_aliases=aliases,
    )


def move(own):
    half = own.shape[0] // 2
    own, head = together(own, own[:half])
    first = lax.ppermute(head, ("side", "core"), [(2, 0), (3, 2)])
    second = lax.ppermute(own[half:], ("side", "core"), [(2, 1)])
    return first, second


def from_side(base, extra):
    group = 2 * lax.axis_index("side") + lax.axis_index("core")
    half = extra.shape[0]
    first = lax.ppermute(extra, ("side", "core"), [(0, 2), (2, 3)])
    second = lax.ppermute(extra, ("side", "core"), [(1, 2)])
    top = jnp.where(group < 2, base[:half], first)
    bottom = jnp.where(group < 2, base[half:], jnp.where(group == 2, second, extra))
    return jnp.concatenate([top, bottom], axis=0)


def outer_halves(value):
    half = value.shape[0] // 2
    return value[:half], value[half:]


def inner_halves(value):
    rows, columns = value.shape
    value = value.reshape(2, 2, rows // 4, columns)
    return value[:, 0].reshape(-1, columns), value[:, 1].reshape(-1, columns)


def join_inner(mine, got):
    rows, columns = mine.shape
    blocks = [v.reshape(2, 1, rows // 2, columns) for v in (mine, got)]
    return jnp.concatenate(blocks, axis=1).reshape(2 * rows, columns)


def across(value, axis, flip):
    pairs = [(i, (i ^ 2) ^ flip) for i in range(4)]
    return lax.ppermute(value, ("side", axis), pairs)


def stage_axes(bits, stage):
    if stage < 2:
        return bits[stage], bits[1 - stage]
    return bits[stage], bits[stage]


def halve(parts, stats, bits):
    parts, stats = list(parts), list(stats)
    for stage in range(len(bits) - 1):
        axes = stage_axes(bits, stage)
        kept, sent = [None, None], [None, None]
        for i in range(2):
            inner = i == 1 and stage == 0
            kept[i], sent[i] = (inner_halves if inner else outer_halves)(parts[i])
            sent[i] = jnp.concatenate([sent[i], stats[i]], axis=0)
        sent = together(*sent)
        got = [swap(sent[i], axes[i]) for i in range(2)]
        got = together(*got)
        for i in range(2):
            rows = kept[i].shape[0]
            parts[i] = kept[i] + got[i][:rows]
            stats[i] = stats[i] + got[i][rows:]
    return parts, stats


def last_messages(part, stats):
    kept, sent = outer_halves(part)
    return jnp.concatenate([kept, stats], axis=0), jnp.concatenate([sent, stats], axis=0)


def reduce_moment(held, statistics, bits):
    half = held.shape[1] // 2
    parts, stats = halve(
        (held[:, :half], held[:, half:]),
        (statistics[:, :half], statistics[:, half:]),
        bits,
    )
    statistics = jnp.concatenate(stats, axis=1)
    kept, sent = together(*last_messages(jnp.concatenate(parts, axis=1), statistics))
    straight, crossed = together(across(kept, bits[-1], 0), across(sent, bits[-1], 1))
    return statistics, straight + crossed


def reduce_mixed(crossing, staying, cross_stats, stay_stats, bits):
    parts, stats = halve((crossing, staying), (cross_stats, stay_stats), bits)
    kept, sent = last_messages(parts[0], stats[0])
    stay_kept, stay_sent = last_messages(parts[1], stats[1])
    kept, sent, stay_sent = together(kept, sent, stay_sent)
    got = (
        across(kept, bits[-1], 0),
        across(sent, bits[-1], 1),
        swap(stay_sent, bits[-1]),
    )
    straight, crossed, got = together(*got)
    second = lax.axis_index("side") == 1
    return straight + crossed + jnp.where(second, stay_kept + got, 0.0)


def gather_moment(own, facing, bits):
    rows = facing.shape[0] - PAD
    chunk, facing = facing[:rows], facing[rows:]
    if own is None:
        chunk, facing = together(chunk, facing)
        got, own = together(swap(chunk, bits[-1]), swap(facing, "side"))
    else:
        got = swap(jnp.concatenate([chunk, own], axis=0), bits[-1])
        got, own = got[:rows], own + got[rows:]
    both = jnp.concatenate([own, facing], axis=0)
    value = jnp.concatenate([chunk, got], axis=0)
    half = value.shape[1] // 2
    parts = [value[:, :half], value[:, half:]]
    for stage in reversed(range(len(bits) - 1)):
        axes = stage_axes(bits, stage)
        if stage == 0:
            *parts, both = together(*parts, both)
            got = [swap(parts[i], axes[i]) for i in range(2)]
            *got, peer = together(*got, swap(both, "core"))
        else:
            parts = together(*parts)
            got = together(*(swap(parts[i], axes[i]) for i in range(2)))
        joined = []
        for i in range(2):
            if i == 1 and stage == 0:
                joined.append(join_inner(parts[i], got[i]))
            else:
                joined.append(jnp.concatenate([parts[i], got[i]], axis=0))
        parts = joined
    both = both + peer
    return jnp.concatenate(parts, axis=1), both[:PAD], both[PAD:]


def weigh(logits, mass, squares, totals):
    scaled = jax.nn.softmax(logits, axis=1) * mass
    columns = jnp.sum(scaled, axis=0, keepdims=True)
    sums = [jnp.sum(scaled * squares, axis=0, keepdims=True), columns]
    if totals:
        total = in_lanes(jnp.sum(scaled, axis=1, keepdims=True), columns.shape[1])
        sums.append(jnp.sum(total, axis=0, keepdims=True))
    rest = PAD - len(sums)
    return scaled, jnp.concatenate([*sums, jnp.zeros((rest, columns.shape[1]))], axis=0)


def make_body(axes):
    bits = axes[2:][::-1]

    def body(points, log_factor, masses):
        return steps(points, log_factor, masses)

    def steps(points, log_factor, masses):
        source = lax.axis_index("side") == 0
        group = 2 * lax.axis_index("side") + lax.axis_index("core")
        rows, _ = points.shape
        rank = log_factor.shape[1]
        half = rows // 2
        devices = 1
        for axis in axes:
            devices *= lax.axis_size(axis)

        moved = move(points)
        mass = masses[:, None]
        near, far, far_base, squares = arrange_base(points, bits)
        lanes = lax.broadcasted_iota(jnp.int32, (rows, 128), 1)
        packed = jnp.concatenate(
            [log_factor, jnp.where(lanes < 64, mass, squares)], axis=1
        )

        second_core = lax.axis_index("core") == 1
        scaled, statistics = weigh(log_factor, mass, squares, True)
        stay_stats = jnp.where(group == 2, statistics, 0.0)
        statistics = jnp.where(group == 2, 0.0, statistics)
        other = swap(contract_rows(far_base, scaled), "core")
        held, other = together(contract_rows(near[:rows], scaled), other)
        crossing = jnp.where(
            source, held + other, jnp.where(second_core, held, other)
        )
        staying = jnp.where(second_core, other, held)
        facing = reduce_mixed(crossing, staying, statistics, stay_stats, bits)
        moment, own, facing = gather_moment(None, facing, bits)

        first, second = move(packed)
        extra = jnp.where(group == 1, second, jnp.where(group == 3, packed[half:], first))
        near, far = arrange_extra(points, *moved, near, far, bits)
        logits = jnp.concatenate([log_factor, extra[:, :rank]], axis=0)
        mass = jnp.concatenate(
            [jnp.where(source, mass, 0.0), extra[:, rank : rank + 1]], axis=0
        )
        squares = jnp.concatenate([squares, extra[:, rank + 64 : rank + 65]], axis=0)
        real = source | (lax.broadcasted_iota(jnp.int32, (logits.shape[0], 1), 0) >= rows)

        own_mass, mass_total = own[2:3], facing[2:3]
        for iteration in range(ITERS):
            if iteration:
                scaled, statistics = weigh(logits, mass, squares, False)
                other = swap(contract_rows(far, scaled), "core")
                held, other = together(contract_rows(near, scaled), other)
                own, facing = reduce_moment(held + other, statistics, bits)
                moment, own, facing = gather_moment(own, facing, bits)
            cross, other = together(times(near, moment), swap(moment, "core"))
            cross = cross + times(far, other)
            share = facing[1:2] / mass_total
            marginal = 0.5 * (own[1:2] / own_mass + share)
            gradient = (
                squares * share - 2.0 * (cross / mass_total) + facing[0:1] / mass_total
            ) / marginal
            centred = gradient - jnp.mean(gradient, axis=1, keepdims=True)
            largest = jnp.max(jnp.where(real, jnp.abs(centred), 0.0), axis=1, keepdims=True)
            largest = jnp.max(in_lanes(largest, 128), axis=0, keepdims=True)
            spread = jnp.broadcast_to(largest, (devices, 128))
            largest = jnp.max(lax.all_to_all(spread, axes, 0, 0, tiled=True), axis=0)
            rate = jnp.tile(step_scale / (largest + 1e-06), rank // 128)
            logits = logits - rate[None, :] * gradient
        factors = rank * jax.nn.softmax(logits, axis=1)
        return from_side(factors[:rows], factors[rows:])

    return body


def solution(mesh):
    pts = mesh.shape["pts"]
    count = pts.bit_length() - 1
    axes = ("side", "core") + tuple(f"bit{i}" for i in reversed(range(count)))
    split = Mesh(mesh.devices.reshape((2,) * len(axes)), axes)
    in_specs = (P(axes, None), P(axes, None), P(axes))
    return jax.shard_map(
        make_body(axes), mesh=split, in_specs=in_specs, out_specs=P(axes, None), check_vma=False
    )
```

```python
import functools

import jax
import jax.numpy as jnp
from jax import lax
from jax.experimental import pallas as pl
from jax.experimental.pallas import tpu as pltpu
from jax.sharding import Mesh, PartitionSpec as P


ITERS = 2

step_scale = 4.0
highest = lax.Precision.HIGHEST
PAD = 8


def swap(value, axis):
    return lax.ppermute(value, axis, [(0, 1), (1, 0)])


def together(*values):
    return lax.optimization_barrier(values)


def in_lanes(column, lanes):
    return lax.optimization_barrier(jnp.broadcast_to(column, (column.shape[0], lanes)))


def contract_rows(left, right):
    return lax.dot_general(
        left,
        right,
        (((0,), (0,)), ((), ())),
        precision=highest,
        preferred_element_type=jnp.float32,
    )


def times(left, right):
    return jnp.dot(left, right, precision=highest, preferred_element_type=jnp.float32)


def own_place(bits):
    place = lax.axis_index("core")
    for axis in bits:
        place = 2 * place + lax.axis_index(axis)
    return place


def column_copies(source, begin, parts, place, sems):
    count = sems.shape[0]
    width = source.shape[1] // count
    rows = parts[0].shape[0]
    copies = []
    for i in range(count):
        column = pl.multiple_of((i ^ place) * width, width)
        copies.append(
            pltpu.make_async_copy(
                source.at[pl.ds(begin, rows), pl.ds(column, width)],
                parts[2 * i // count].at[:, pl.ds(i % (count // 2) * width, width)],
                sems.at[i],
            )
        )
    return copies


def row_copies(parts, targets, top, sems):
    rows = parts[0].shape[0]
    return [
        pltpu.make_async_copy(parts[i], targets[i].at[pl.ds(top, rows), :], sems.at[i])
        for i in range(2)
    ]


def base_kernel(bits, points, near, far, far_part, squares, near_part, sems, out_sems):
    parts = near_part, far_part
    copies = column_copies(points, 0, parts, own_place(bits), sems)
    for copy in copies:
        copy.start()
    for copy in copies:
        copy.wait()
    copies = row_copies(parts, (near, far), 0, out_sems)
    for copy in copies:
        copy.start()
    total = jnp.zeros_like(squares)
    for part in parts:
        for begin in range(0, part.shape[1], 128):
            block = part[:, begin : begin + 128]
            total = total + block * block
    squares[...] = total
    for copy in copies:
        copy.wait()


def extra_kernel(
    bits, points, first, second, near_in, far_in, near, far, near_part, far_part, sems, out_sems
):
    del near_in, far_in
    parts = near_part, far_part
    place = own_place(bits)
    group = 2 * lax.axis_index("side") + lax.axis_index("core")
    half = first.shape[0]

    @pl.when((group == 0) | (group == 2))
    def _():
        for copy in column_copies(first, 0, parts, place, sems):
            copy.start()

    @pl.when(group == 1)
    def _():
        for copy in column_copies(second, 0, parts, place, sems):
            copy.start()

    @pl.when(group == 3)
    def _():
        for copy in column_copies(points, half, parts, place, sems):
            copy.start()

    for copy in column_copies(first, 0, parts, place, sems):
        copy.wait()
    copies = row_copies(parts, (near, far), points.shape[0], out_sems)
    for copy in copies:
        copy.start()
    for copy in copies:
        copy.wait()


def arrange_base(points, bits):
    rows, width = points.shape
    blocks = 2 ** (1 + len(bits))
    if (width // blocks) % 128:
        near, far = reorder(points, bits)
        return near, far, far, jnp.sum(points * points, axis=1, keepdims=True)
    anywhere = pl.BlockSpec(memory_space=pl.ANY)
    inside = pl.BlockSpec(memory_space=pltpu.VMEM)
    whole = pltpu.HBM((rows + rows // 2, width // 2), points.dtype)
    part = pltpu.VMEM((rows, width // 2), points.dtype)
    *arrays, sums = pl.pallas_call(
        functools.partial(base_kernel, bits),
        out_shape=(whole, whole, part, pltpu.VMEM((rows, 128), points.dtype)),
        in_specs=[anywhere],
        out_specs=(anywhere, anywhere, inside, inside),
        scratch_shapes=[
            part,
            pltpu.SemaphoreType.DMA((blocks,)),
            pltpu.SemaphoreType.DMA((2,)),
        ],
        compiler_params=pltpu.CompilerParams(vmem_limit_bytes=4 << 20),
        name="base_rows",
    )(pltpu.with_memory_space_constraint(points, pltpu.HBM))
    return *arrays, jnp.sum(sums, axis=1, keepdims=True)


def reorder(points, bits):
    rows, width = points.shape
    blocks = 2 ** (1 + len(bits))
    order = jnp.arange(blocks) ^ own_place(bits)
    whole = points.reshape(rows, blocks, -1)[:, order].reshape(rows, width)
    return whole[:, : width // 2], whole[:, width // 2 :]


def arrange_extra(points, first, second, near, far, bits):
    rows, width = points.shape
    blocks = 2 ** (1 + len(bits))
    half = rows // 2
    if (width // blocks) % 128:
        group = 2 * lax.axis_index("side") + lax.axis_index("core")
        extra = jnp.where(group == 1, second, jnp.where(group == 3, points[half:], first))
        extra = reorder(extra, bits)
        return tuple(jnp.concatenate(pair, axis=0) for pair in zip((near, far), extra))
    return arrange_call(extra_kernel, points, half, bits, {3: 0, 4: 1})(
        pltpu.with_memory_space_constraint(points, pltpu.HBM), first, second, near, far
    )


def arrange_call(kernel, points, count, bits, aliases):
    rows, width = points.shape
    anywhere = pl.BlockSpec(memory_space=pl.ANY)
    shape = jax.ShapeDtypeStruct((rows + rows // 2, width // 2), points.dtype)
    part = pltpu.VMEM((count, width // 2), points.dtype)
    return pl.pallas_call(
        functools.partial(kernel, bits),
        out_shape=(shape, shape),
        in_specs=[anywhere] * 5,
        out_specs=(anywhere, anywhere),
        scratch_shapes=[
            part,
            part,
            pltpu.SemaphoreType.DMA((2 ** (1 + len(bits)),)),
            pltpu.SemaphoreType.DMA((2,)),
        ],
        input_output_aliases=aliases,
    )


def move(own):
    half = own.shape[0] // 2
    own, head = together(own, own[:half])
    first = lax.ppermute(head, ("side", "core"), [(2, 0), (3, 2)])
    second = lax.ppermute(own[half:], ("side", "core"), [(2, 1)])
    return first, second


def from_side(base, extra):
    group = 2 * lax.axis_index("side") + lax.axis_index("core")
    half = extra.shape[0]
    first = lax.ppermute(extra, ("side", "core"), [(0, 2), (2, 3)])
    second = lax.ppermute(extra, ("side", "core"), [(1, 2)])
    top = jnp.where(group < 2, base[:half], first)
    bottom = jnp.where(group < 2, base[half:], jnp.where(group == 2, second, extra))
    return jnp.concatenate([top, bottom], axis=0)


def outer_halves(value):
    half = value.shape[0] // 2
    return value[:half], value[half:]


def inner_halves(value):
    rows, columns = value.shape
    value = value.reshape(2, 2, rows // 4, columns)
    return value[:, 0].reshape(-1, columns), value[:, 1].reshape(-1, columns)


def join_inner(mine, got):
    rows, columns = mine.shape
    blocks = [v.reshape(2, 1, rows // 2, columns) for v in (mine, got)]
    return jnp.concatenate(blocks, axis=1).reshape(2 * rows, columns)


def across(value, axis, flip):
    pairs = [(i, (i ^ 2) ^ flip) for i in range(4)]
    return lax.ppermute(value, ("side", axis), pairs)


def stage_axes(bits, stage):
    if stage < 2:
        return bits[stage], bits[1 - stage]
    return bits[stage], bits[stage]


def halve(parts, stats, bits):
    parts, stats = list(parts), list(stats)
    for stage in range(len(bits) - 1):
        axes = stage_axes(bits, stage)
        kept, sent = [None, None], [None, None]
        for i in range(2):
            inner = i == 1 and stage == 0
            kept[i], sent[i] = (inner_halves if inner else outer_halves)(parts[i])
            sent[i] = jnp.concatenate([sent[i], stats[i]], axis=0)
        sent = together(*sent)
        got = [swap(sent[i], axes[i]) for i in range(2)]
        got = together(*got)
        for i in range(2):
            rows = kept[i].shape[0]
            parts[i] = kept[i] + got[i][:rows]
            stats[i] = stats[i] + got[i][rows:]
    return parts, stats


def last_messages(part, stats):
    kept, sent = outer_halves(part)
    return jnp.concatenate([kept, stats], axis=0), jnp.concatenate([sent, stats], axis=0)


def reduce_moment(held, statistics, bits):
    half = held.shape[1] // 2
    parts, stats = halve(
        (held[:, :half], held[:, half:]),
        (statistics[:, :half], statistics[:, half:]),
        bits,
    )
    chunk = parts[0].shape[0] // 2
    whole = jnp.concatenate(
        [jnp.concatenate(parts, axis=1), jnp.concatenate(stats, axis=1)], axis=0
    )
    crossed, straight = together(across(whole, bits[-1], 1), across(whole, bits[-1], 0))
    value = jnp.concatenate(
        [straight[:chunk] + crossed[chunk : 2 * chunk], straight[chunk : 2 * chunk] + crossed[:chunk]],
        axis=0,
    )
    return value, straight[2 * chunk :] + crossed[2 * chunk :]


def reduce_mixed(crossing, staying, cross_stats, stay_stats, bits):
    parts, stats = halve((crossing, staying), (cross_stats, stay_stats), bits)
    kept, sent = last_messages(parts[0], stats[0])
    stay_kept, stay_sent = last_messages(parts[1], stats[1])
    kept, sent, stay_sent = together(kept, sent, stay_sent)
    got = (
        across(sent, bits[-1], 1),
        swap(stay_sent, bits[-1]),
        across(kept, bits[-1], 0),
    )
    crossed, got, straight = together(*got)
    second = lax.axis_index("side") == 1
    return straight + crossed + jnp.where(second, stay_kept + got, 0.0)


def gather_last(facing, bits):
    rows = facing.shape[0] - PAD
    chunk, facing = together(facing[:rows], facing[rows:])
    got, own = together(swap(chunk, bits[-1]), swap(facing, "side"))
    return jnp.concatenate([chunk, got], axis=0), own, facing


def gather_moment(value, own, facing, bits):
    both = jnp.concatenate([own, facing], axis=0)
    half = value.shape[1] // 2
    parts = [value[:, :half], value[:, half:]]
    for stage in reversed(range(len(bits) - 1)):
        axes = stage_axes(bits, stage)
        if stage == 0:
            *parts, both = together(*parts, both)
            got = [swap(parts[i], axes[i]) for i in range(2)]
            *got, peer = together(*got, swap(both, "core"))
        else:
            parts = together(*parts)
            got = together(*(swap(parts[i], axes[i]) for i in range(2)))
        joined = []
        for i in range(2):
            if i == 1 and stage == 0:
                joined.append(join_inner(parts[i], got[i]))
            else:
                joined.append(jnp.concatenate([parts[i], got[i]], axis=0))
        parts = joined
    both = both + peer
    return jnp.concatenate(parts, axis=1), both[:PAD], both[PAD:]


def weigh(logits, mass, squares, totals):
    scaled = jax.nn.softmax(logits, axis=1) * mass
    columns = jnp.sum(scaled, axis=0, keepdims=True)
    sums = [jnp.sum(scaled * squares, axis=0, keepdims=True), columns]
    if totals:
        total = in_lanes(jnp.sum(scaled, axis=1, keepdims=True), columns.shape[1])
        sums.append(jnp.sum(total, axis=0, keepdims=True))
    rest = PAD - len(sums)
    return scaled, jnp.concatenate([*sums, jnp.zeros((rest, columns.shape[1]))], axis=0)


def make_body(axes):
    bits = axes[2:][::-1]

    def body(points, log_factor, masses):
        return steps(points, log_factor, masses)

    def steps(points, log_factor, masses):
        source = lax.axis_index("side") == 0
        group = 2 * lax.axis_index("side") + lax.axis_index("core")
        rows, _ = points.shape
        rank = log_factor.shape[1]
        half = rows // 2
        devices = 1
        for axis in axes:
            devices *= lax.axis_size(axis)

        moved = move(points)
        mass = masses[:, None]
        near, far, far_base, squares = arrange_base(points, bits)
        lanes = lax.broadcasted_iota(jnp.int32, (rows, 128), 1)
        packed = jnp.concatenate(
            [log_factor, jnp.where(lanes < 64, mass, squares)], axis=1
        )

        second_core = lax.axis_index("core") == 1
        scaled, statistics = weigh(log_factor, mass, squares, True)
        stay_stats = jnp.where(group == 2, statistics, 0.0)
        statistics = jnp.where(group == 2, 0.0, statistics)
        other = swap(contract_rows(far_base, scaled), "core")
        held, other = together(contract_rows(near[:rows], scaled), other)
        crossing = jnp.where(
            source, held + other, jnp.where(second_core, held, other)
        )
        staying = jnp.where(second_core, other, held)
        facing = reduce_mixed(crossing, staying, statistics, stay_stats, bits)
        moment, own, facing = gather_moment(*gather_last(facing, bits), bits)

        first, second = move(packed)
        extra = jnp.where(group == 1, second, jnp.where(group == 3, packed[half:], first))
        near, far = arrange_extra(points, *moved, near, far, bits)
        logits = jnp.concatenate([log_factor, extra[:, :rank]], axis=0)
        mass = jnp.concatenate(
            [jnp.where(source, mass, 0.0), extra[:, rank : rank + 1]], axis=0
        )
        squares = jnp.concatenate([squares, extra[:, rank + 64 : rank + 65]], axis=0)
        real = source | (lax.broadcasted_iota(jnp.int32, (logits.shape[0], 1), 0) >= rows)

        own_mass, mass_total = own[2:3], facing[2:3]
        for iteration in range(ITERS):
            if iteration:
                scaled, statistics = weigh(logits, mass, squares, False)
                other = swap(contract_rows(far, scaled), "core")
                held, other = together(contract_rows(near, scaled), other)
                value, facing = reduce_moment(held + other, statistics, bits)
                own = swap(facing, "side")
                moment, own, facing = gather_moment(value, own, facing, bits)
            cross, other = together(times(near, moment), swap(moment, "core"))
            cross = cross + times(far, other)
            share = facing[1:2] / mass_total
            marginal = 0.5 * (own[1:2] / own_mass + share)
            gradient = (
                squares * share - 2.0 * (cross / mass_total) + facing[0:1] / mass_total
            ) / marginal
            centred = gradient - jnp.mean(gradient, axis=1, keepdims=True)
            largest = jnp.max(jnp.where(real, jnp.abs(centred), 0.0), axis=1, keepdims=True)
            largest = jnp.max(in_lanes(largest, 128), axis=0, keepdims=True)
            spread = jnp.broadcast_to(largest, (devices, 128))
            largest = jnp.max(lax.all_to_all(spread, axes, 0, 0, tiled=True), axis=0)
            rate = jnp.tile(step_scale / (largest + 1e-06), rank // 128)
            logits = logits - rate[None, :] * gradient
        factors = rank * jax.nn.softmax(logits, axis=1)
        return from_side(factors[:rows], factors[rows:])

    return body


def solution(mesh):
    pts = mesh.shape["pts"]
    count = pts.bit_length() - 1
    axes = ("side", "core") + tuple(f"bit{i}" for i in reversed(range(count)))
    split = Mesh(mesh.devices.reshape((2,) * len(axes)), axes)
    in_specs = (P(axes, None), P(axes, None), P(axes))
    return jax.shard_map(
        make_body(axes), mesh=split, in_specs=in_specs, out_specs=P(axes, None), check_vma=False
    )
```
